256 devices in a mesh: node: 32 (over z, x_lo, core), term: 8 (over x_hi, y).
Axes of the slice: x: 4 (x_hi: 2, x_lo: 2; x = x_hi * 2 + x_lo), y: 4, z: 8, core: 2. Of those that a mesh axis runs over, the one named last changes fastest.
Arguments:
- node_tensors: bfloat16 [32, 64, 4096], P('node'), may hold values from -0.046875 to 1.046875
- prim_ops: bfloat16 [32, 32, 2, 64, 64], P('node', 'term'), may hold values from -3.8 to 3.8, as said below
- active: int32 [32, 32, 2], P('node', 'term'), may hold values 0 or 1
- top_field: bfloat16 [32, 64, 64], P('term'), may hold values from -0.95 to 0.95, as said below
- node_map: int32 [32], replicated, may hold values from 0 to 31, as said below
Outputs:
- derivative: bfloat16 [32, 64, 4096], P('node', 'term')
The draws below stay inside these ranges and needn't reach their ends.
Inputs may be any that keep to these rules, and one draw needn't show every extreme that they name: node_map holds every position 0 to 31 once; position 31 is no node; the slot of position 1 is the slot of position 0 plus 32 // 2, counted round. `prim_ops`: each operator is symmetric. `top_field`: each matrix is symmetric.
All inputs are finite; a program needn't handle non-finite values. No bound on the sum of `active` on one device may be relied on, other than what follows from the above.
Results may differ from the reference program's by a relative error of at most 0.025.
The reference program's roundings to bfloat16 on the way count: a program that leaves them out, or rounds other values in their place, can miss the bound.
Values may be sent and summed in bfloat16 or wider, within the bound.
A program may use at most 64 MiB of HBM per device.

```python
import jax
import jax.numpy as jnp
from jax import lax

B = 64
TERM_DEV = 4
TERMS = 32
SLOTS = 32


def draw_node_tensors(key, part):
    key_noise = jax.random.fold_in(key, 11)
    key_place = jax.random.fold_in(key, 12)
    noise = jax.random.truncated_normal(key_noise, -4.0, 4.0, (SLOTS, B * B, B), jnp.float32) * (0.7 / B)
    place_keys = jax.random.split(key_place, SLOTS)
    chosen = jax.vmap(lambda single: jax.random.permutation(single, B * B)[:B])(place_keys)
    cells = jnp.arange(B * B, dtype=jnp.int32)
    aligned = (cells[None, :, None] == chosen[:, None, :]).astype(jnp.float32)
    return (aligned + noise).reshape(SLOTS, B, B * B).astype(jnp.bfloat16)


def draw_prim_ops(key, part):
    key_main = jax.random.fold_in(key, 21)
    raw = jax.random.truncated_normal(key_main, -4.0, 4.0, (SLOTS, TERMS, 2, B, B), jnp.float32)
    return ((raw + jnp.swapaxes(raw, -1, -2)) * (0.67 / 1.4143)).astype(jnp.bfloat16)


def draw_top_field(key, part):
    key_main = jax.random.fold_in(key, 31)
    raw = jax.random.truncated_normal(key_main, -4.0, 4.0, (TERMS, B, B), jnp.float32)
    return ((raw + jnp.swapaxes(raw, -1, -2)) * (0.16 / 1.4143)).astype(jnp.bfloat16)


def draw_node_map(key, part):
    key_main = jax.random.fold_in(key, 41)
    shuffled = jax.random.permutation(key_main, SLOTS).astype(jnp.int32)
    slot_ids = jnp.arange(SLOTS, dtype=jnp.int32)
    root_slot = jnp.sum(jnp.where(shuffled == 0, slot_ids, 0))
    target = (root_slot + SLOTS // 2) % SLOTS
    displaced = jnp.sum(jnp.where(slot_ids == target, shuffled, 0))
    moved = jnp.where(shuffled == 1, displaced, shuffled)
    return jnp.where(slot_ids == target, 1, moved).astype(jnp.int32)


def plant(entries, key, least, top_value):
    longest = entries.shape.index(max(entries.shape))
    spots = []
    for shift in (0, 1):
        where = [jax.random.randint(jax.random.fold_in(key, axis), (), 0, length) for axis, length in enumerate(entries.shape)]
        where[longest] = (where[longest] + shift) % entries.shape[longest]
        spots.append(tuple(where))
    return entries.at[spots[0]].set(least).at[spots[1]].set(top_value)


def setup_inputs(seed: int = 0) -> dict:
    splits = jax.random.split(jax.random.key(seed), 6)
    return {
        "node_tensors": draw_node_tensors(jax.random.fold_in(splits[5], 71), 0),
        "prim_ops": draw_prim_ops(jax.random.fold_in(splits[5], 71), 0),
        "active": plant((jax.random.randint(splits[2], (SLOTS, TERMS, 2), 0, 4) < 3).astype(jnp.int32), jax.random.fold_in(splits[2], 1), 0, 1),
        "top_field": draw_top_field(jax.random.fold_in(splits[5], 71), 0),
        "node_map": draw_node_map(jax.random.fold_in(splits[5], 71), 0),
    }


def mode_one(matrix, tensor):
    extent = tensor.shape[0]
    return jnp.dot(matrix, tensor.reshape(extent, -1), preferred_element_type=jnp.float32).reshape(tensor.shape)


def mode_two(matrix, tensor):
    return jnp.einsum("ij,ajc->aic", matrix.astype(jnp.float32), tensor.astype(jnp.float32))


def mode_three(matrix, tensor):
    extent = tensor.shape[2]
    return jnp.dot(tensor.reshape(-1, extent), matrix.T, preferred_element_type=jnp.float32).reshape(tensor.shape)


def up_term(tensor, left_term, right_term):
    extent = tensor.shape[2]
    partial_one = mode_two(right_term, tensor).astype(jnp.bfloat16)
    weighted = mode_one(left_term, partial_one).astype(jnp.bfloat16)
    return jnp.dot(tensor.reshape(-1, extent).T, weighted.reshape(-1, extent), preferred_element_type=jnp.float32).astype(jnp.bfloat16)


def down_term(tensor, left_term, right_term, field_now):
    extent = tensor.shape[0]
    reduced = mode_three(field_now, tensor).astype(jnp.bfloat16)
    side_left = mode_two(right_term, reduced).astype(jnp.bfloat16)
    side_right = mode_one(left_term, reduced).astype(jnp.bfloat16)
    field_left = jnp.dot(tensor.reshape(extent, -1), side_left.reshape(extent, -1).T, preferred_element_type=jnp.float32).astype(jnp.bfloat16)
    field_right = jnp.einsum("abc,adc->bd", tensor.astype(jnp.float32), side_right.astype(jnp.float32)).astype(jnp.bfloat16)
    deriv_term = mode_one(left_term, side_left)
    return field_left, field_right, deriv_term


def reference(node_tensors, prim_ops, active, top_field, node_map):
    slots = node_map.shape[0]
    count = slots - 1
    first_leaf = count // 2
    extent = node_tensors.shape[1]
    terms_all = top_field.shape[0]
    groups = terms_all // TERM_DEV
    inverse = jnp.zeros((slots,), jnp.int32).at[node_map].set(jnp.arange(slots, dtype=jnp.int32))
    identity = jnp.eye(extent, dtype=jnp.bfloat16)

    def tensor_at(place):
        return node_tensors[inverse[place]].reshape(extent, extent, extent)

    def children_of(place, term_mats):
        if place >= first_leaf:
            slot_here = inverse[place]
            operators = jnp.where(active[slot_here][..., None, None] == 1, prim_ops[slot_here], identity)
            return operators[:, 0], operators[:, 1]
        return term_mats[2 * place + 1], term_mats[2 * place + 2]

    term_mats = {}
    for place in range(count - 1, 0, -1):
        tensor_here = tensor_at(place)
        left_terms, right_terms = children_of(place, term_mats)
        term_mats[place] = lax.map(lambda pair: up_term(tensor_here, pair[0], pair[1]), (left_terms, right_terms))

    fields = {0: top_field}
    result = jnp.zeros((slots, extent, extent * extent), jnp.bfloat16)
    for place in range(count):
        tensor_here = tensor_at(place)
        left_terms, right_terms = children_of(place, term_mats)
        field_here = fields[place]

        def group_step(total, items):
            parts = jnp.zeros((extent, extent, extent), jnp.float32)
            lefts = []
            rights = []
            for inner in range(TERM_DEV):
                field_left, field_right, deriv_term = down_term(tensor_here, items[0][inner], items[1][inner], items[2][inner])
                parts = parts + deriv_term
                lefts.append(field_left)
                rights.append(field_right)
            rounded = lax.optimization_barrier(parts.astype(jnp.bfloat16))
            return total + rounded.astype(jnp.float32), (jnp.stack(lefts), jnp.stack(rights))

        shaped = (left_terms.reshape(groups, TERM_DEV, extent, extent),
                  right_terms.reshape(groups, TERM_DEV, extent, extent),
                  field_here.reshape(groups, TERM_DEV, extent, extent))
        total, (lefts_all, rights_all) = lax.scan(group_step, jnp.zeros((extent, extent, extent), jnp.float32), shaped)
        if place < first_leaf:
            fields[2 * place + 1] = lefts_all.reshape(terms_all, extent, extent)
            fields[2 * place + 2] = rights_all.reshape(terms_all, extent, extent)
        result = result.at[inverse[place]].set(total.astype(jnp.bfloat16).reshape(extent, extent * extent))
    return result
```

```python
import functools

import jax
import jax.numpy as jnp
from jax import lax
from jax.experimental import pallas as pl
from jax.experimental.pallas import tpu as pltpu
from jax.sharding import PartitionSpec as P

MESH = pl.DeviceIdType.MESH
F32 = jnp.float32
BF16 = jnp.bfloat16
LEVELS = 4


def mm(x, y):
    return lax.dot_general(x, y, (((1,), (0,)), ((), ())), preferred_element_type=F32)


def mm_nt(x, y):
    return lax.dot_general(x, y, (((1,), (1,)), ((), ())), preferred_element_type=F32)


def iota(shape, dim):
    return lax.broadcasted_iota(jnp.int32, shape, dim)


def kernel(
    n_term,
    tbl,
    a1,
    a1p,
    a3,
    an2,
    an2p,
    leaf,
    top,
    out,
    e_r,
    e_l,
    j_r,
    j_l,
    m_r,
    m_l,
    m_m,
    perm,
    x_buf,
    y_buf,
    w_buf,
    ra_buf,
    la_buf,
    v_buf,
    bd_buf,
    lr_buf,
    m_buf,
    pieces,
    rs,
    *rest,
):
    zbuf = rest[0:4]
    psend = rest[4:8]
    prbuf = rest[8:12]
    dpl = rest[12:16]
    zsend = rest[16:20]
    zr = rest[20:24]
    us, ur, ps, pr, ds_, dr, zs, zr_sem, ts, tr = rest[24:34]

    node = lax.axis_index("node")
    term = lax.axis_index("term")
    z = node // 4
    j = lax.rem(node, 4)

    def at_node(zt, jt):
        return {"node": zt * 4 + jt}

    partners = []
    for dz in range(1, 8):
        partners.append(at_node(lax.rem(z + dz, 8), j))
    for dj in range(1, 4):
        partners.append(at_node(z, lax.rem(j + dj, 4)))
    for dt in range(1, n_term):
        partners.append({"term": lax.rem(term + dt, n_term)})
    barrier = pltpu.get_barrier_semaphore()
    for partner in partners:
        pl.semaphore_signal(barrier, inc=1, device_id=partner, device_id_type=MESH)

    rows, cols = iota((256, 64), 0), iota((256, 64), 1)
    by, bx = rows // 16, lax.rem(rows // 4, 4)
    e_r[...] = jnp.where(cols == bx * 16 + by, 1.0, 0.0).astype(BF16)
    e_l[...] = jnp.where(cols == lax.rem(rows, 64), 1.0, 0.0).astype(BF16)
    rows, cols = iota((128, 256), 0), iota((128, 256), 1)
    for half in range(2):
        k = rows - 64 * half
        j_r[half] = jnp.where(k == lax.rem(cols, 64), 1.0, 0.0).astype(BF16)
        j_l[half] = jnp.where(k == (cols // 16) * 4 + lax.rem(cols, 4), 1.0, 0.0).astype(BF16)
    rows, cols = iota((256, 256), 0), iota((256, 256), 1)
    m_r[...] = jnp.where(lax.rem(rows, 4) == cols // 64, 1.0, 0.0)
    same_bx = rows // 64 == lax.rem(cols // 4, 4)
    m_l[...] = jnp.where(same_bx, 1.0, 0.0)
    m_m[...] = jnp.where(rows // 64 == cols // 64, 1.0, 0.0)
    same_a = lax.rem(rows, 64) == (cols // 16) * 4 + lax.rem(cols, 4)
    perm[...] = jnp.where(same_bx & same_a, 1.0, 0.0).astype(BF16)
    low = iota((16, 128), 1) < 64
    low64 = iota((64, 128), 1) < 64

    def expand(pair, half, e, jm, mask):
        spread = mm(e[...], pair).astype(BF16)
        return (mm(spread, jm[half]) * mask[...]).astype(BF16)

    def op_on_mid(src, side, dst):
        def body(rp, _):
            pair = lr_buf[side, pl.ds(pl.multiple_of(rp * 64, 64), 64), :]
            for half in range(2):
                weight = expand(pair, half, e_r, j_r, m_r)
                r = rp * 2 + half
                for g in range(4):
                    o = mm(weight, src[:, g * 256 : (g + 1) * 256])
                    for k in range(2):
                        for i in range(8):
                            u = o[32 * i : 32 * i + 16, 128 * k : 128 * k + 128]
                            v = o[32 * i + 16 : 32 * i + 32, 128 * k : 128 * k + 128]
                            ur_, vr_ = pltpu.roll(u, 64, 1), pltpu.roll(v, 64, 1)
                            hi = (4 * g + 2 * k) * 16
                            lanes = slice(i * 128, i * 128 + 128)
                            dst[r, hi : hi + 16, lanes] = jnp.where(low, u, vr_).astype(BF16)
                            dst[r, hi + 16 : hi + 32, lanes] = jnp.where(low, ur_, v).astype(BF16)
            return 0

        lax.fori_loop(0, 2, body, 0)

    def up(send):
        op_on_mid(a1, 1, x_buf)

        def body(rp, _):
            span = pl.ds(pl.multiple_of(rp * 64, 64), 64)
            pair = lr_buf[0, span, :]
            both = []
            for half in range(2):
                weight = expand(pair, half, e_l, j_l, m_l)
                r = rp * 2 + half
                acc = jnp.zeros((256, 256), F32)
                for g in range(4):
                    w = mm(weight, x_buf[r, :, g * 256 : (g + 1) * 256]).astype(BF16)
                    acc = acc + mm(a3[g], w)
                s = jnp.where(low64, acc[0:64, 0:128], acc[64:128, 0:128]) + jnp.where(
                    low64, acc[128:192, 128:256], acc[192:256, 128:256]
                )
                both.append(s + pltpu.roll(s, 64, 1))
            send[z, span, :] = jnp.where(low64, both[0], both[1]).astype(BF16)
            return 0

        lax.fori_loop(0, 2, body, 0)

    def natural(src, dst):
        def body(r, _):
            for g in range(4):
                lanes = slice(g * 256, g * 256 + 256)
                dst[r, :, lanes] = mm(perm[...], src[r, :, lanes]).astype(BF16)
            return 0

        lax.fori_loop(0, 4, body, 0)

    def weighted():
        def body(rp, _):
            pair = lr_buf[0, pl.ds(pl.multiple_of(rp * 64, 64), 64), :]
            for half in range(2):
                weight = expand(pair, half, e_l, j_l, m_l)
                r = rp * 2 + half
                for g in range(4):
                    lanes = slice(g * 256, g * 256 + 256)
                    w_buf[r, :, lanes] = mm(weight, x_buf[r, :, lanes]).astype(BF16)
            return 0

        lax.fori_loop(0, 2, body, 0)

    def field():
        def body(rp, _):
            pair = m_buf[pl.ds(pl.multiple_of(rp * 64, 64), 64), :]
            for half in range(2):
                bd_buf[rp * 2 + half] = expand(pair, half, e_l, j_r, m_m)
            return 0

        lax.fori_loop(0, 2, body, 0)

    def down(src, base, dst, slot):
        def body(r, _):
            span = pl.ds(pl.multiple_of(r * 64, 64), 64)
            for g in range(4):
                lanes = slice(g * 256, g * 256 + 256)
                v = mm(src[r, :, lanes], bd_buf[r]).astype(BF16)
                for q in range(4):
                    v_buf[q, span, lanes] = v[q * 64 : q * 64 + 64]
            return 0

        lax.fori_loop(0, 4, body, 0)
        acc = jnp.zeros((256, 128), F32)
        for q in range(4):
            acc = acc + mm_nt(v_buf[q], base[:, q * 1024 : q * 1024 + 1024])
        for rp in range(2):
            dst[slot, rp * 64 : rp * 64 + 64, :] = jnp.where(
                low64, acc[rp * 128 : rp * 128 + 64], acc[rp * 128 + 64 : rp * 128 + 128]
            ).astype(BF16)

    pending = []
    for level in range(LEVELS):
        prbuf[level][4] = leaf[...]
    for level in range(LEVELS):
        zr[level][8] = top[...]

    lr_buf[...] = leaf[...]
    for level in range(LEVELS):
        zb, sb, rb = zbuf[level], psend[level], prbuf[level]
        up(zb)
        if level == 0:
            pl.semaphore_wait(barrier, len(partners))
        copies = []
        for dz in (4, 3, 5, 2, 6, 1, 7):
            copy = pltpu.make_async_remote_copy(
                src_ref=zb.at[z],
                dst_ref=zb.at[z],
                send_sem=us.at[level * 8 + dz],
                recv_sem=ur.at[level * 8 + dz],
                device_id=at_node(lax.rem(z + dz, 8), j),
                device_id_type=MESH,
            )
            copy.start()
            copies.append(copy)
        for copy in copies:
            copy.wait_recv()
        pending += copies
        copies = []
        for dj in (1, 2, 3, 0):
            if dj == 0:
                rb[j, 0] = zb[tbl[0]]
                rb[j, 1] = zb[tbl[1]]
                continue
            sb[dj, 0] = zb[tbl[2 * dj]]
            sb[dj, 1] = zb[tbl[2 * dj + 1]]
            copy = pltpu.make_async_remote_copy(
                src_ref=sb.at[dj],
                dst_ref=rb.at[j],
                send_sem=ps.at[level * 4 + dj],
                recv_sem=pr.at[level * 4 + dj],
                device_id=at_node(z, lax.rem(j + dj, 4)),
                device_id_type=MESH,
            )
            copy.start()
            copies.append(copy)
        for copy in copies:
            copy.wait_recv()
        pending += copies
        lr_buf[0] = rb[tbl[8], 0]
        lr_buf[1] = rb[tbl[9], 1]

    m_buf[...] = top[...]
    op_on_mid(a1, 1, x_buf)
    natural(x_buf, ra_buf)
    op_on_mid(a1p, 0, y_buf)
    natural(y_buf, la_buf)

    for level in range(LEVELS):
        db, sb, rb = dpl[level], zsend[level], zr[level]
        field()
        down(ra_buf, an2, db, 2 * j)
        down(la_buf, an2p, db, 2 * j + 1)
        copies = []
        for dj in (1, 2, 3):
            copy = pltpu.make_async_remote_copy(
                src_ref=db.at[pl.ds(2 * j, 2)],
                dst_ref=db.at[pl.ds(2 * j, 2)],
                send_sem=ds_.at[level * 4 + dj],
                recv_sem=dr.at[level * 4 + dj],
                device_id=at_node(z, lax.rem(j + dj, 4)),
                device_id_type=MESH,
            )
            copy.start()
            copies.append(copy)
        if level == 0:
            weighted()
        for copy in copies:
            copy.wait_recv()
        pending += copies
        copies = []
        for dz in (4, 3, 5, 2, 6, 1, 7, 0):
            if dz == 0:
                rb[z] = db[tbl[10]]
                continue
            sb[dz] = db[tbl[10 + dz]]
            copy = pltpu.make_async_remote_copy(
                src_ref=sb.at[dz],
                dst_ref=rb.at[z],
                send_sem=zs.at[level * 8 + dz],
                recv_sem=zr_sem.at[level * 8 + dz],
                device_id=at_node(lax.rem(z + dz, 8), j),
                device_id_type=MESH,
            )
            copy.start()
            copies.append(copy)
        for copy in copies:
            copy.wait_recv()
        pending += copies
        m_buf[...] = rb[tbl[18]]

    field()
    height = 64 // n_term

    def last(g, _):
        lanes = pl.ds(pl.multiple_of(g * 256, 256), 256)
        acc = jnp.zeros((256, 256), F32)
        for r in range(4):
            acc = acc + mm(w_buf[r, :, lanes], bd_buf[r])
        for q in range(4):
            span = pl.ds(pl.multiple_of(q * 1024 + g * 256, 256), 256)
            for t in range(n_term):
                first = q * 64 + t * height
                pieces[t, :, span] = acc[first : first + height].astype(BF16)
        return 0

    lax.fori_loop(0, 4, last, 0)
    copies = []
    for dt in range(1, n_term):
        target = lax.rem(term + dt, n_term)
        copy = pltpu.make_async_remote_copy(
            src_ref=pieces.at[target],
            dst_ref=rs.at[dt],
            send_sem=ts.at[dt],
            recv_sem=tr.at[dt],
            device_id={"term": target},
            device_id_type=MESH,
        )
        copy.start()
        copies.append(copy)
    total = pieces[term].astype(F32)
    for copy in copies:
        copy.wait_recv()
    for dt in range(1, n_term):
        total = total + rs[dt].astype(F32)
    out[...] = total.astype(BF16)
    pending += copies
    for copy in pending:
        copy.wait_send()


def pairs(mats):
    lead = mats.shape[:-3]
    x = mats.reshape(lead + (2, 2, 64, 64))
    return jnp.swapaxes(x, -3, -2).reshape(lead + (128, 128))


def per_device(n_term, node_tensors, prim_ops, active, top_field, node_map):
    node = lax.axis_index("node")
    z, j = node // 4, node % 4
    tensor = node_tensors[0].reshape(64, 64, 64)
    swapped = jnp.swapaxes(tensor, 0, 1)

    def split(x):
        return x.reshape(16, 4, 64, 64).transpose(1, 2, 0, 3).reshape(256, 1024)

    a1 = split(tensor)
    a1p = split(swapped)
    a3 = tensor.reshape(64, 4, 4, 4, 64).transpose(2, 3, 4, 1, 0).reshape(4, 256, 256)
    flat, flatp = tensor.reshape(64, 4096), swapped.reshape(64, 4096)
    an2 = jnp.concatenate([flat, flat], axis=0)
    an2p = jnp.concatenate([flatp, flatp], axis=0)
    identity = jnp.eye(64, dtype=BF16)
    leaf = jnp.where(active[0][..., None, None] == 1, prim_ops[0], identity)
    leaf = pairs(jnp.swapaxes(leaf, 0, 1))
    top = pairs(top_field)

    slots = jnp.arange(32, dtype=jnp.int32)

    def slot_of(positions):
        return jnp.sum(jnp.where(node_map[None, :] == positions[:, None], slots[None, :], 0), axis=1)

    mates = z * 4 + (j + jnp.arange(4)) % 4
    mate_pos = node_map[mates]
    left, right = slot_of(2 * mate_pos + 1), slot_of(2 * mate_pos + 2)
    plane = jnp.stack([left // 4, right // 4], axis=1).reshape(8)
    is_leaf = mate_pos[0] >= 15
    own = jnp.stack([jnp.where(is_leaf, 4, left[0] % 4), jnp.where(is_leaf, 4, right[0] % 4)])
    ring = ((z + jnp.arange(8)) % 8) * 4 + j
    ring_pos = node_map[ring]
    parent = slot_of((ring_pos - 1) // 2)
    pick = (parent % 4) * 2 + (1 - ring_pos % 2)
    from_z = jnp.where(ring_pos[:1] == 0, 8, parent[:1] // 4)
    tbl = jnp.concatenate([plane, own, pick, from_z]).astype(jnp.int32)

    vmem = pl.BlockSpec(memory_space=pltpu.VMEM)
    height = 64 // n_term
    dma = pltpu.SemaphoreType.DMA
    scratch = [
        pltpu.VMEM((256, 64), BF16),
        pltpu.VMEM((256, 64), BF16),
        pltpu.VMEM((2, 128, 256), BF16),
        pltpu.VMEM((2, 128, 256), BF16),
        pltpu.VMEM((256, 256), F32),
        pltpu.VMEM((256, 256), F32),
        pltpu.VMEM((256, 256), F32),
        pltpu.VMEM((256, 256), BF16),
        pltpu.VMEM((4, 256, 1024), BF16),
        pltpu.VMEM((4, 256, 1024), BF16),
        pltpu.VMEM((4, 256, 1024), BF16),
        pltpu.VMEM((4, 256, 1024), BF16),
        pltpu.VMEM((4, 256, 1024), BF16),
        pltpu.VMEM((4, 256, 1024), BF16),
        pltpu.VMEM((4, 256, 256), BF16),
        pltpu.VMEM((2, 128, 128), BF16),
        pltpu.VMEM((128, 128), BF16),
        pltpu.VMEM((n_term, height, 4096), BF16),
        pltpu.VMEM((n_term, height, 4096), BF16),
    ]
    scratch += [pltpu.VMEM((8, 128, 128), BF16)] * 4
    scratch += [pltpu.VMEM((4, 2, 128, 128), BF16)] * 4
    scratch += [pltpu.VMEM((5, 2, 128, 128), BF16)] * 4
    scratch += [pltpu.VMEM((8, 128, 128), BF16)] * 4
    scratch += [pltpu.VMEM((8, 128, 128), BF16)] * 4
    scratch += [pltpu.VMEM((9, 128, 128), BF16)] * 4
    scratch += [dma((32,)), dma((32,)), dma((16,)), dma((16,)), dma((16,)), dma((16,)), dma((32,)), dma((32,)), dma((8,)), dma((8,))]
    result = pl.pallas_call(
        functools.partial(kernel, n_term),
        out_shape=jax.ShapeDtypeStruct((height, 4096), BF16),
        in_specs=[pl.BlockSpec(memory_space=pltpu.SMEM)] + [vmem] * 7,
        out_specs=vmem,
        scratch_shapes=scratch,
        compiler_params=pltpu.CompilerParams(
            collective_id=0, has_side_effects=True, vmem_limit_bytes=60 * 1024 * 1024
        ),
    )(tbl, a1, a1p, a3, an2, an2p, leaf, top)
    return jnp.where(node_map[node] == 31, jnp.zeros_like(result), result)[None]


def solution(mesh):
    placed = (
        P("node", None, None),
        P("node", "term", None, None, None),
        P("node", "term", None),
        P("term", None, None),
        P(),
    )
    return jax.shard_map(
        functools.partial(per_device, mesh.shape["term"]),
        mesh=mesh,
        in_specs=placed,
        out_specs=P("node", "term", None),
        check_vma=False,
    )
```

```python
import functools

import jax
import jax.numpy as jnp
from jax import lax
from jax.experimental import pallas as pl
from jax.experimental.pallas import tpu as pltpu
from jax.sharding import PartitionSpec as P

MESH = pl.DeviceIdType.MESH
F32 = jnp.float32
BF16 = jnp.bfloat16
LEVELS = 4


def mm(x, y):
    return lax.dot_general(x, y, (((1,), (0,)), ((), ())), preferred_element_type=F32)


def mm_nt(x, y):
    return lax.dot_general(x, y, (((1,), (1,)), ((), ())), preferred_element_type=F32)


def iota(shape, dim):
    return lax.broadcasted_iota(jnp.int32, shape, dim)


def kernel(
    n_term,
    node_map,
    active,
    tensor,
    prim,
    top_field,
    out,
    nb,
    swb,
    a3,
    an2,
    an2p,
    e_r,
    e_l,
    j_r,
    j_l,
    m_r,
    m_l,
    m_m,
    perm,
    x_buf,
    y_buf,
    w_buf,
    ra_buf,
    la_buf,
    v_buf,
    bd_buf,
    lr_buf,
    m_buf,
    pieces,
    rs,
    *rest,
):
    zbuf, psend, prbuf, dpl, zsend, zr = (rest[8 * k : 8 * k + 8] for k in range(6))
    us, ur, ps, pr, ds_, dr, zs, zr_sem, ts, tr = rest[48:58]

    node = lax.axis_index("node")
    term = lax.axis_index("term")
    z = node // 4
    j = lax.rem(node, 4)

    def at_node(zt, jt):
        return {"node": zt * 4 + jt}

    partners = []
    for dz in range(1, 8):
        partners.append(at_node(lax.rem(z + dz, 8), j))
    for dj in range(1, 4):
        partners.append(at_node(z, lax.rem(j + dj, 4)))
    for dt in range(1, n_term):
        partners.append({"term": lax.rem(term + dt, n_term)})
    barrier = pltpu.get_barrier_semaphore()
    for partner in partners:
        pl.semaphore_signal(barrier, inc=1, device_id=partner, device_id_type=MESH)

    rows, cols = iota((256, 64), 0), iota((256, 64), 1)
    by, bx = rows // 16, lax.rem(rows // 4, 4)
    e_r[...] = jnp.where(cols == bx * 16 + by, 1.0, 0.0).astype(BF16)
    e_l[...] = jnp.where(cols == lax.rem(rows, 64), 1.0, 0.0).astype(BF16)
    rows, cols = iota((128, 256), 0), iota((128, 256), 1)
    for half in range(2):
        k = rows - 64 * half
        j_r[half] = jnp.where(k == lax.rem(cols, 64), 1.0, 0.0).astype(BF16)
        j_l[half] = jnp.where(k == lax.rem(cols, 4) * 16 + cols // 16, 1.0, 0.0).astype(BF16)
    rows, cols = iota((256, 256), 0), iota((256, 256), 1)
    m_r[...] = jnp.where(lax.rem(rows, 4) == cols // 64, 1.0, 0.0)
    same_bx = rows // 64 == lax.rem(cols // 4, 4)
    m_l[...] = jnp.where(same_bx, 1.0, 0.0)
    m_m[...] = jnp.where(rows // 64 == cols // 64, 1.0, 0.0)
    same_a = lax.rem(rows, 64) == lax.rem(cols, 4) * 16 + cols // 16
    perm[...] = jnp.where(same_bx & same_a, 1.0, 0.0).astype(BF16)
    same_lo = lax.rem(rows, 4) == cols // 64
    same_t = lax.rem(cols, 64) == lax.rem(rows // 4, 4) * 16 + rows // 16
    unit = jnp.where(same_lo & same_t, 1.0, 0.0).astype(BF16)
    eye = jnp.where(rows == cols, 1.0, 0.0).astype(BF16)
    eye64 = jnp.where(iota((64, 64), 0) == iota((64, 64), 1), 1.0, 0.0).astype(BF16)
    low = iota((16, 128), 1) < 64
    low64 = iota((64, 128), 1) < 64

    def expand(pair, half, e, jm, mask):
        spread = mm(e[...], pair).astype(BF16)
        return (mm(spread, jm[half]) * mask[...]).astype(BF16)

    def spread_mid(weight, src, dst, r):
        for g in range(4):
            o = mm(weight, src[:, g * 256 : (g + 1) * 256])
            for k in range(2):
                for i in range(8):
                    u = o[32 * i : 32 * i + 16, 128 * k : 128 * k + 128]
                    v = o[32 * i + 16 : 32 * i + 32, 128 * k : 128 * k + 128]
                    ur_, vr_ = pltpu.roll(u, 64, 1), pltpu.roll(v, 64, 1)
                    hi = (4 * g + 2 * k) * 16
                    lanes = slice(i * 128, i * 128 + 128)
                    dst[r, hi : hi + 16, lanes] = jnp.where(low, u, vr_).astype(BF16)
                    dst[r, hi + 16 : hi + 32, lanes] = jnp.where(low, ur_, v).astype(BF16)

    def op_on_mid(src, side, dst, hp):
        pair = lr_buf[hp, side]
        for half in range(2):
            spread_mid(expand(pair, half, e_r, j_r, m_r), src, dst, hp * 2 + half)

    def up(send, hp):
        op_on_mid(swb, 1, x_buf, hp)
        pair = lr_buf[hp, 0]
        both = []
        for half in range(2):
            weight = expand(pair, half, e_l, j_l, m_l)
            acc = jnp.zeros((256, 256), F32)
            for g in range(4):
                w = mm(weight, x_buf[hp * 2 + half, :, g * 256 : (g + 1) * 256]).astype(BF16)
                acc = acc + mm(a3[g], w)
            s = jnp.where(low64, acc[0:64, 0:128], acc[64:128, 0:128]) + jnp.where(
                low64, acc[128:192, 128:256], acc[192:256, 128:256]
            )
            both.append(s + pltpu.roll(s, 64, 1))
        send[z] = jnp.where(low64, both[0], both[1]).astype(BF16)

    def natural(src, dst, hp):
        for r in (2 * hp, 2 * hp + 1):
            for g in range(4):
                lanes = slice(g * 256, g * 256 + 256)
                dst[r, :, lanes] = mm(perm[...], src[r, :, lanes]).astype(BF16)

    def weighted(hp):
        for half in range(2):
            weight = expand(lr_buf[hp, 0], half, e_l, j_l, m_l)
            r = hp * 2 + half
            for g in range(4):
                lanes = slice(g * 256, g * 256 + 256)
                w_buf[r, :, lanes] = mm(weight, x_buf[r, :, lanes]).astype(BF16)

    def field(hp):
        for half in range(2):
            bd_buf[hp * 2 + half] = expand(m_buf[hp], half, e_l, j_r, m_m)

    def down(src, base, dst, slot, hp):
        for half in range(2):
            r = 2 * hp + half
            for g in range(4):
                lanes = slice(g * 256, g * 256 + 256)
                v = mm(src[r, :, lanes], bd_buf[r]).astype(BF16)
                for q in range(4):
                    v_buf[hp, q, half * 64 : half * 64 + 64, lanes] = v[q * 64 : q * 64 + 64]
        acc = jnp.zeros((128, 128), F32)
        for q in range(4):
            acc = acc + mm_nt(v_buf[hp, q], base[:, q * 1024 : q * 1024 + 1024])
        dst[slot] = jnp.where(low64, acc[0:64], acc[64:128]).astype(BF16)

    for q in range(4):
        nb[q * 64 : q * 64 + 64] = tensor[:, q * 1024 : q * 1024 + 1024]
    an2[0:64] = tensor[...]
    an2[64:128] = tensor[...]
    for g in range(4):
        a3[g] = mm_nt(eye, nb[:, g * 256 : g * 256 + 256]).astype(BF16)
    spread_mid(unit, nb, y_buf, 0)
    for g in range(4):
        lanes = slice(g * 256, g * 256 + 256)
        swb[:, lanes] = mm(perm[...], y_buf[0, :, lanes]).astype(BF16)
    for q in range(4):
        for dup in range(2):
            an2p[dup * 64 : dup * 64 + 64, q * 1024 : q * 1024 + 1024] = swb[q * 64 : q * 64 + 64]
    for hp in range(2):
        for side in range(2):
            ops = []
            for r in (2 * hp, 2 * hp + 1):
                acts = jnp.full((64, 64), active[r, side], jnp.int32) == 1
                ops.append(jnp.where(acts, prim[0, r, side], eye64))
            lr_buf[hp, side] = jnp.concatenate(ops, axis=1)
        m_buf[hp] = jnp.concatenate([top_field[2 * hp], top_field[2 * hp + 1]], axis=1)
        for level in range(LEVELS):
            prbuf[2 * level + hp][4] = lr_buf[hp]
            zr[2 * level + hp][8] = m_buf[hp]

    def own_slot(k):
        return z * 4 + lax.rem(j + k, 4)

    mates = [node_map[own_slot(k)] for k in range(4)]
    ring = [node_map[lax.rem(z + k, 8) * 4 + j] for k in range(8)]
    wanted = [2 * p + 1 for p in mates] + [2 * p + 2 for p in mates]

    def find(slot, found):
        here = node_map[slot]
        below = [jnp.where(here == want, slot, old) for want, old in zip(wanted, found[:8])]
        kids = (2 * here + 1, 2 * here + 2)
        above = [
            jnp.where((kids[0] == p) | (kids[1] == p), slot, old) for p, old in zip(ring, found[8:])
        ]
        return tuple(below + above)

    found = lax.fori_loop(0, 32, find, tuple(jnp.int32(0) for _ in range(16)))
    is_leaf = mates[0] >= 15
    tbl = []
    for k in range(4):
        tbl += [found[k] // 4, found[4 + k] // 4]
    tbl += [jnp.where(is_leaf, 4, lax.rem(found[side], 4)) for side in (0, 4)]
    tbl += [lax.rem(up_slot, 4) * 2 + 1 - lax.rem(p, 2) for up_slot, p in zip(found[8:], ring)]
    tbl.append(jnp.where(mates[0] == 0, 8, found[8] // 4))

    pending = []
    flight = {}

    def send(key, sems, slot, src, dst, to):
        copy = pltpu.make_async_remote_copy(
            src_ref=src,
            dst_ref=dst,
            send_sem=sems[0].at[slot],
            recv_sem=sems[1].at[slot],
            device_id=to,
            device_id_type=MESH,
        )
        copy.start()
        flight.setdefault(key, []).append(copy)
        pending.append(copy)

    def arrived(key):
        for copy in flight.pop(key):
            copy.wait_recv()

    def to_ring(dz):
        return at_node(lax.rem(z + dz, 8), j)

    def to_mate(dj):
        return at_node(z, lax.rem(j + dj, 4))

    def up_start(n):
        zb = zbuf[n]
        for dz in (4, 3, 5, 2, 6, 1, 7):
            send(("uz", n), (us, ur), n * 8 + dz, zb.at[z], zb.at[z], to_ring(dz))

    def up_relay(n):
        zb, sb, rb = zbuf[n], psend[n], prbuf[n]
        arrived(("uz", n))
        for dj in (2, 3, 1):
            sb[dj, 0] = zb[tbl[2 * dj]]
            sb[dj, 1] = zb[tbl[2 * dj + 1]]
            send(("up", n), (ps, pr), n * 4 + dj, sb.at[dj], rb.at[j], to_mate(dj))
        rb[j, 0] = zb[tbl[0]]
        rb[j, 1] = zb[tbl[1]]

    def up_finish(n):
        arrived(("up", n))
        lr_buf[n % 2, 0] = prbuf[n][tbl[8], 0]
        lr_buf[n % 2, 1] = prbuf[n][tbl[9], 1]

    for level in range(LEVELS):
        for hp in range(2):
            n = 2 * level + hp
            if level > 0:
                up_finish(n - 2)
            up(zbuf[n], hp)
            if n == 0:
                pl.semaphore_wait(barrier, len(partners))
            up_start(n)
        up_relay(2 * level)
        up_relay(2 * level + 1)

    def down_start(n):
        db = dpl[n]
        own = db.at[pl.ds(2 * j, 2)]
        for dj in (2, 3, 1):
            send(("dp", n), (ds_, dr), n * 4 + dj, own, own, to_mate(dj))

    def down_relay(n):
        db, sb, rb = dpl[n], zsend[n], zr[n]
        arrived(("dp", n))
        for dz in (4, 3, 5, 2, 6, 1, 7):
            sb[dz] = db[tbl[10 + dz]]
            send(("dz", n), (zs, zr_sem), n * 8 + dz, sb.at[dz], rb.at[z], to_ring(dz))
        rb[z] = db[tbl[10]]

    def down_finish(n):
        arrived(("dz", n))
        m_buf[n % 2] = zr[n][tbl[18]]

    for level in range(LEVELS):
        for hp in range(2):
            n = 2 * level + hp
            if level > 0:
                down_finish(n - 2)
            else:
                up_finish(2 * LEVELS - 2 + hp)
                op_on_mid(swb, 1, x_buf, hp)
                natural(x_buf, ra_buf, hp)
                op_on_mid(nb, 0, y_buf, hp)
                natural(y_buf, la_buf, hp)
            field(hp)
            down(ra_buf, an2, dpl[n], 2 * j, hp)
            down(la_buf, an2p, dpl[n], 2 * j + 1, hp)
            down_start(n)
        down_relay(2 * level)
        down_relay(2 * level + 1)
        if level == 0:
            weighted(0)
            weighted(1)

    for hp in range(2):
        down_finish(2 * LEVELS - 2 + hp)
        field(hp)
    height = 64 // n_term

    def last(g, _):
        lanes = pl.ds(pl.multiple_of(g * 256, 256), 256)
        acc = jnp.zeros((256, 256), F32)
        for r in range(4):
            acc = acc + mm(w_buf[r, :, lanes], bd_buf[r])
        for q in range(4):
            span = pl.ds(pl.multiple_of(q * 1024 + g * 256, 256), 256)
            for t in range(n_term):
                first = q * 64 + t * height
                pieces[t, :, span] = acc[first : first + height].astype(BF16)
        return 0

    lax.fori_loop(0, 4, last, 0)
    for dt in range(1, n_term):
        target = lax.rem(term + dt, n_term)
        send("t", (ts, tr), dt, pieces.at[target], rs.at[dt], {"term": target})
    total = pieces[term].astype(F32)
    if n_term > 1:
        arrived("t")
    for dt in range(1, n_term):
        total = total + rs[dt].astype(F32)
    absent = jnp.full(total.shape, mates[0], jnp.int32) == 31
    out[...] = jnp.where(absent, 0.0, total).astype(BF16)
    for copy in pending:
        copy.wait_send()


def per_device(n_term, node_tensors, prim_ops, active, top_field, node_map):
    vmem = pl.BlockSpec(memory_space=pltpu.VMEM)
    height = 64 // n_term
    dma = pltpu.SemaphoreType.DMA
    scratch = [
        pltpu.VMEM((256, 1024), BF16),
        pltpu.VMEM((256, 1024), BF16),
        pltpu.VMEM((4, 256, 256), BF16),
        pltpu.VMEM((128, 4096), BF16),
        pltpu.VMEM((128, 4096), BF16),
        pltpu.VMEM((256, 64), BF16),
        pltpu.VMEM((256, 64), BF16),
        pltpu.VMEM((2, 128, 256), BF16),
        pltpu.VMEM((2, 128, 256), BF16),
        pltpu.VMEM((256, 256), F32),
        pltpu.VMEM((256, 256), F32),
        pltpu.VMEM((256, 256), F32),
        pltpu.VMEM((256, 256), BF16),
        pltpu.VMEM((4, 256, 1024), BF16),
        pltpu.VMEM((4, 256, 1024), BF16),
        pltpu.VMEM((4, 256, 1024), BF16),
        pltpu.VMEM((4, 256, 1024), BF16),
        pltpu.VMEM((4, 256, 1024), BF16),
        pltpu.VMEM((2, 4, 128, 1024), BF16),
        pltpu.VMEM((4, 256, 256), BF16),
        pltpu.VMEM((2, 2, 64, 128), BF16),
        pltpu.VMEM((2, 64, 128), BF16),
        pltpu.VMEM((n_term, height, 4096), BF16),
        pltpu.VMEM((n_term, height, 4096), BF16),
    ]
    for lead in ((8,), (4, 2), (5, 2), (8,), (8,), (9,)):
        scratch += [pltpu.VMEM(lead + (64, 128), BF16)] * (2 * LEVELS)
    scratch += [dma((count,)) for count in (64, 64, 32, 32, 32, 32, 64, 64, 8, 8)]
    result = pl.pallas_call(
        functools.partial(kernel, n_term),
        out_shape=jax.ShapeDtypeStruct((height, 4096), BF16),
        in_specs=[pl.BlockSpec(memory_space=pltpu.SMEM)] * 2 + [vmem] * 3,
        out_specs=vmem,
        scratch_shapes=scratch,
        compiler_params=pltpu.CompilerParams(
            collective_id=0, has_side_effects=True, vmem_limit_bytes=60 * 1024 * 1024
        ),
    )(node_map, active[0], node_tensors[0], prim_ops, top_field)
    return result[None]


def solution(mesh):
    placed = (
        P("node", None, None),
        P("node", "term", None, None, None),
        P("node", "term", None),
        P("term", None, None),
        P(),
    )
    return jax.shard_map(
        functools.partial(per_device, mesh.shape["term"]),
        mesh=mesh,
        in_specs=placed,
        out_specs=P("node", "term", None),
        check_vma=False,
    )
```

```python
import functools

import jax
import jax.numpy as jnp
from jax import lax
from jax.experimental import pallas as pl
from jax.experimental.pallas import tpu as pltpu
from jax.sharding import PartitionSpec as P

MESH = pl.DeviceIdType.MESH
F32 = jnp.float32
BF16 = jnp.bfloat16
LEVELS = 4


def mm(x, y):
    return lax.dot_general(x, y, (((1,), (0,)), ((), ())), preferred_element_type=F32)


def mm_nt(x, y):
    return lax.dot_general(x, y, (((1,), (1,)), ((), ())), preferred_element_type=F32)


def iota(shape, dim):
    return lax.broadcasted_iota(jnp.int32, shape, dim)


def kernel(
    n_term,
    node_map,
    inverse,
    active,
    tensor,
    prim,
    top_field,
    out,
    nb,
    swb,
    a3,
    e_r,
    e_l,
    j_r,
    j_l,
    m_r,
    m_l,
    m_m,
    perm,
    unit,
    x_buf,
    y_buf,
    w_buf,
    v_buf,
    bd_buf,
    lr_buf,
    sib_buf,
    m_buf,
    blk,
    sa_buf,
    za,
    pa_send,
    pa,
    ta_send,
    ta,
    pieces,
    rs,
    *rest,
):
    zbuf, psend, prbuf = (rest[8 * k : 8 * k + 8] for k in range(3))
    us, ur, ps, pr, azs, azr, aps, apr, ats, atr, ts, tr = rest[24:36]

    node = lax.axis_index("node")
    term = lax.axis_index("term")
    z = node // 4
    j = lax.rem(node, 4)

    def at_node(zt, jt):
        return {"node": zt * 4 + jt}

    partners = []
    for dz in range(1, 8):
        partners.append(at_node(lax.rem(z + dz, 8), j))
    for dj in range(1, 4):
        partners.append(at_node(z, lax.rem(j + dj, 4)))
    for dt in range(1, n_term):
        partners.append({"term": lax.rem(term + dt, n_term)})
    barrier = pltpu.get_barrier_semaphore()
    for partner in partners:
        pl.semaphore_signal(barrier, inc=1, device_id=partner, device_id_type=MESH)

    rows, cols = iota((256, 64), 0), iota((256, 64), 1)
    by, bx = rows // 16, lax.rem(rows // 4, 4)
    e_r[...] = jnp.where(cols == bx * 16 + by, 1.0, 0.0).astype(BF16)
    e_l[...] = jnp.where(cols == lax.rem(rows, 64), 1.0, 0.0).astype(BF16)
    rows, cols = iota((128, 256), 0), iota((128, 256), 1)
    for half in range(2):
        k = rows - 64 * half
        j_r[half] = jnp.where(k == lax.rem(cols, 64), 1.0, 0.0).astype(BF16)
        j_l[half] = jnp.where(k == lax.rem(cols, 4) * 16 + cols // 16, 1.0, 0.0).astype(BF16)
    rows, cols = iota((256, 256), 0), iota((256, 256), 1)
    m_r[...] = jnp.where(lax.rem(rows, 4) == cols // 64, 1.0, 0.0)
    same_bx = rows // 64 == lax.rem(cols // 4, 4)
    m_l[...] = jnp.where(same_bx, 1.0, 0.0)
    m_m[...] = jnp.where(rows // 64 == cols // 64, 1.0, 0.0)
    same_a = lax.rem(rows, 64) == lax.rem(cols, 4) * 16 + cols // 16
    perm[...] = jnp.where(same_bx & same_a, 1.0, 0.0).astype(BF16)
    same_lo = lax.rem(rows, 4) == cols // 64
    same_t = lax.rem(cols, 64) == lax.rem(rows // 4, 4) * 16 + rows // 16
    unit[...] = jnp.where(same_lo & same_t, 1.0, 0.0).astype(BF16)
    eye = jnp.where(rows == cols, 1.0, 0.0).astype(BF16)
    eye64 = jnp.where(iota((64, 64), 0) == iota((64, 64), 1), 1.0, 0.0).astype(BF16)
    low = iota((16, 128), 1) < 64
    low64 = iota((64, 128), 1) < 64

    def expand(pair, half, e, jm, mask):
        spread = mm(e[...], pair).astype(BF16)
        return (mm(spread, jm[half]) * mask[...]).astype(BF16)

    def spread_mid(weight, src, dst, r):
        for g in range(4):
            o = mm(weight, src(slice(g * 256, g * 256 + 256)))
            for k in range(2):
                for i in range(8):
                    u = o[32 * i : 32 * i + 16, 128 * k : 128 * k + 128]
                    v = o[32 * i + 16 : 32 * i + 32, 128 * k : 128 * k + 128]
                    ur_, vr_ = pltpu.roll(u, 64, 1), pltpu.roll(v, 64, 1)
                    hi = (4 * g + 2 * k) * 16
                    lanes = slice(i * 128, i * 128 + 128)
                    dst[r, hi : hi + 16, lanes] = jnp.where(low, u, vr_).astype(BF16)
                    dst[r, hi + 16 : hi + 32, lanes] = jnp.where(low, ur_, v).astype(BF16)

    def op_on_mid(src, side, dst, hp):
        pair = lr_buf[hp, side]
        for half in range(2):
            weight = expand(pair, half, e_r, j_r, m_r)
            spread_mid(weight, lambda lanes: src[:, lanes], dst, hp * 2 + half)

    def up(send, hp):
        op_on_mid(swb, 1, x_buf, hp)
        pair = lr_buf[hp, 0]
        both = []
        for half in range(2):
            weight = expand(pair, half, e_l, j_l, m_l)
            acc = jnp.zeros((256, 256), F32)
            for g in range(4):
                w = mm(weight, x_buf[hp * 2 + half, :, g * 256 : (g + 1) * 256]).astype(BF16)
                acc = acc + mm(a3[g], w)
            s = jnp.where(low64, acc[0:64, 0:128], acc[64:128, 0:128]) + jnp.where(
                low64, acc[128:192, 128:256], acc[192:256, 128:256]
            )
            both.append(s + pltpu.roll(s, 64, 1))
        send[z] = jnp.where(low64, both[0], both[1]).astype(BF16)

    def natural(src, r, dst):
        for g in range(4):
            lanes = slice(g * 256, g * 256 + 256)
            dst[:, lanes] = mm(perm[...], src[r, :, lanes]).astype(BF16)

    def weighted(hp):
        for half in range(2):
            weight = expand(lr_buf[hp, 0], half, e_l, j_l, m_l)
            r = hp * 2 + half
            for g in range(4):
                lanes = slice(g * 256, g * 256 + 256)
                w_buf[r, :, lanes] = mm(weight, x_buf[r, :, lanes]).astype(BF16)

    def field(k, hp):
        pair = m_buf[hp, k]
        for half in range(2):
            bd_buf[hp * 2 + half] = expand(pair, half, e_l, j_r, m_m)

    def walk(k, hp):
        field(k - 1, hp)
        for half in range(2):
            r = 2 * hp + half
            for g in range(4):
                lanes = slice(g * 256, g * 256 + 256)
                v = mm(sa_buf[k - 1, r, :, lanes], bd_buf[r]).astype(BF16)
                for q in range(4):
                    v_buf[hp, q, half * 64 : half * 64 + 64, lanes] = v[q * 64 : q * 64 + 64]
        acc = jnp.zeros((128, 64), F32)
        for q in range(4):
            acc = acc + mm_nt(v_buf[hp, q], blk[k - 1, base_of[k], q * 64 : q * 64 + 64, :])
        m_buf[hp, k] = jnp.concatenate([acc[0:64], acc[64:128]], axis=1).astype(BF16)

    def prepare(k, hp):
        for half in range(2):
            r = 2 * hp + half
            weight = expand(sib_buf[hp, k], half, e_r, j_r, m_r)
            spread_mid(weight, lambda lanes: blk[k - 1, 1 - base_of[k], :, lanes], y_buf, r)
            natural(y_buf, r, sa_buf.at[k - 1, r])

    for q in range(4):
        nb[q * 64 : q * 64 + 64] = tensor[:, q * 1024 : q * 1024 + 1024]
    for g in range(4):
        a3[g] = mm_nt(eye, nb[:, g * 256 : g * 256 + 256]).astype(BF16)
    y_unit = y_buf
    spread_mid(unit[...], lambda lanes: nb[:, lanes], y_unit, 0)
    natural(y_unit, 0, swb)
    for hp in range(2):
        for side in range(2):
            ops = []
            for r in (2 * hp, 2 * hp + 1):
                acts = jnp.full((64, 64), active[r, side], jnp.int32) == 1
                ops.append(jnp.where(acts, prim[0, r, side], eye64))
            lr_buf[hp, side] = jnp.concatenate(ops, axis=1)
        m_buf[hp, 0] = jnp.concatenate([top_field[2 * hp], top_field[2 * hp + 1]], axis=1)

    def slot_of(q):
        return inverse[jnp.maximum(jnp.minimum(q, 32) - 1, 0)]

    def at_depth(q, k):
        return (q >= 2**k) & (q < 2 ** (k + 1))

    def ancestor(q, k):
        best = jnp.int32(1)
        for up_by in range(6):
            best = jnp.where(at_depth(q // 2**up_by, k), q // 2**up_by, best)
        return best

    def sibling(q):
        return q + 1 - 2 * lax.rem(q, 2)

    here = [node_map[z * 4 + lax.rem(j + k, 4)] + 1 for k in range(4)]
    first_of, second_of, tensors_of = [], [], []
    for q in here:
        first_of.append(
            [
                slot_of(jnp.where(at_depth(q, k - 1), 2 * q, sibling(ancestor(q, k))))
                for k in range(1, 5)
            ]
        )
        second_of.append(slot_of(2 * q + 1))
        tensors_of.append([slot_of(ancestor(q, k)) for k in range(4)])
    base_of = [None] + [lax.rem(ancestor(here[0], k), 2) for k in range(1, 5)]
    depth = jnp.int32(0)
    for k in range(1, 5):
        depth = depth + jnp.where(here[0] >= 2**k, 1, 0)

    pending = []
    flight = {}

    def send(key, sems, slot, src, dst, to):
        copy = pltpu.make_async_remote_copy(
            src_ref=src,
            dst_ref=dst,
            send_sem=sems[0].at[slot],
            recv_sem=sems[1].at[slot],
            device_id=to,
            device_id_type=MESH,
        )
        copy.start()
        flight.setdefault(key, []).append(copy)
        pending.append(copy)

    def arrived(key):
        for copy in flight.pop(key):
            copy.wait_recv()

    def to_ring(dz):
        return at_node(lax.rem(z + dz, 8), j)

    def to_mate(dj):
        return at_node(z, lax.rem(j + dj, 4))

    def up_start(n):
        zb = zbuf[n]
        for dz in (4, 3, 5, 2, 6, 1, 7):
            send(("uz", n), (us, ur), n * 8 + dz, zb.at[z], zb.at[z], to_ring(dz))

    def up_relay(n):
        zb, sb, rb = zbuf[n], psend[n], prbuf[n]
        k = LEVELS - 1 - n // 2
        arrived(("uz", n))
        for dj in (2, 3, 1):
            sb[dj, 0] = zb[first_of[dj][k] // 4]
            sb[dj, 1] = zb[second_of[dj] // 4]
            send(("up", n), (ps, pr), n * 4 + dj, sb.at[dj], rb.at[j], to_mate(dj))
        rb[j, 0] = zb[first_of[0][k] // 4]
        rb[j, 1] = zb[second_of[0] // 4]

    def up_finish(n):
        k, hp = LEVELS - 1 - n // 2, n % 2
        rb = prbuf[n]
        rb[4] = lr_buf[hp]
        arrived(("up", n))
        mine = at_depth(here[0], k)
        first = lax.rem(first_of[0][k], 4)
        lr_buf[hp, 0] = rb[jnp.where(mine, first, 4), 0]
        lr_buf[hp, 1] = rb[jnp.where(mine, lax.rem(second_of[0], 4), 4), 1]
        sib_buf[hp, k + 1] = rb[first, 0]

    width = 4096 // n_term
    per_block = 1024 // width

    def fetch_start():
        mine = tensor.at[:, pl.ds(pl.multiple_of(term * width, width), width)]
        for dz in (4, 3, 5, 2, 6, 1, 7):
            send("az", (azs, azr), dz, mine, za.at[z], to_ring(dz))
        za[z] = tensor[:, pl.ds(pl.multiple_of(term * width, width), width)]

    def fetch_relay():
        arrived("az")
        for dj in (2, 3, 1):
            for k in range(4):
                pa_send[dj, k] = za[tensors_of[dj][k] // 4]
            send("ap", (aps, apr), dj, pa_send.at[dj], pa.at[j], to_mate(dj))
        for k in range(4):
            pa[j, k] = za[tensors_of[0][k] // 4]

    def fetch_share():
        arrived("ap")
        for k in range(4):
            ta_send[k] = pa[lax.rem(tensors_of[0][k], 4), k]
        send("ax", (ats, atr), 0, ta_send, ta.at[4], {"term": lax.rem(term + 4, 8)})

    row, column = term // 4, lax.rem(term, 4)

    def fetch_spread(part):
        cut = pl.ds(2 * part, 2)
        if part == 1:
            arrived("ax")
        for dy in (2, 1, 3):
            to = {"term": row * 4 + lax.rem(column + dy, 4)}
            slot = 8 * part + 8 + dy
            send(("at", part), (ats, atr), slot, ta_send.at[cut], ta.at[dy, cut], to)
            send(("at", part), (ats, atr), slot + 4, ta.at[4, cut], ta.at[4 + dy, cut], to)

    def fetch_finish(part):
        arrived(("at", part))
        for dt in range(8):
            source = lax.rem(row + dt // 4, 2) * 4 + lax.rem(column - dt % 4 + 4, 4)
            rows_at = pl.ds(pl.multiple_of((source // per_block) * 64, 64), 64)
            lanes_at = pl.ds(pl.multiple_of(lax.rem(source, per_block) * width, width), width)
            for k in (2 * part, 2 * part + 1):
                blk[k, 0, rows_at, lanes_at] = ta_send[k] if dt == 0 else ta[dt, k]

        def swap(k, _):
            spread_mid(unit[...], lambda lanes: blk[k, 0, :, lanes], y_buf, 0)
            natural(y_buf, 0, blk.at[k, 1])
            return 0

        lax.fori_loop(2 * part, 2 * part + 2, swap, 0)

    for level in range(LEVELS):
        for hp in range(2):
            n = 2 * level + hp
            if level > 0:
                up_finish(n - 2)
            up(zbuf[n], hp)
            if n == 0:
                pl.semaphore_wait(barrier, len(partners))
            up_start(n)
        if level == 0:
            fetch_start()
        if level == 2:
            fetch_spread(1)
        if level == 3:
            fetch_finish(1)
            for hp in range(2):
                prepare(4, hp)
        up_relay(2 * level)
        up_relay(2 * level + 1)
        if level == 0:
            fetch_relay()
        if level == 1:
            fetch_share()
        if level == 2:
            fetch_spread(0)
        if level == 3:
            for hp in range(2):
                prepare(3, hp)
            fetch_finish(0)
            for hp in range(2):
                prepare(2, hp)

    for hp in range(2):
        up_finish(2 * LEVELS - 2 + hp)
        prepare(1, hp)
        op_on_mid(swb, 1, x_buf, hp)
        weighted(hp)
    for k in range(1, 5):
        for hp in range(2):
            walk(k, hp)
    for hp in range(2):
        field(depth, hp)
    height = 64 // n_term

    def last(g, _):
        lanes = pl.ds(pl.multiple_of(g * 256, 256), 256)
        acc = jnp.zeros((256, 256), F32)
        for r in range(4):
            acc = acc + mm(w_buf[r, :, lanes], bd_buf[r])
        for q in range(4):
            span = pl.ds(pl.multiple_of(q * 1024 + g * 256, 256), 256)
            for t in range(n_term):
                first = q * 64 + t * height
                pieces[t, :, span] = acc[first : first + height].astype(BF16)
        return 0

    lax.fori_loop(0, 4, last, 0)
    for dt in range(1, n_term):
        target = lax.rem(term + dt, n_term)
        send("t", (ts, tr), dt, pieces.at[target], rs.at[dt], {"term": target})
    total = pieces[term].astype(F32)
    if n_term > 1:
        arrived("t")
    for dt in range(1, n_term):
        total = total + rs[dt].astype(F32)
    absent = jnp.full(total.shape, here[0], jnp.int32) == 32
    out[...] = jnp.where(absent, 0.0, total).astype(BF16)
    for copy in pending:
        copy.wait_send()


def per_device(n_term, node_tensors, prim_ops, active, top_field, node_map):
    vmem = pl.BlockSpec(memory_space=pltpu.VMEM)
    height = 64 // n_term
    dma = pltpu.SemaphoreType.DMA
    slots = jnp.arange(32, dtype=jnp.int32)
    inverse = jnp.sum(jnp.where(node_map[None, :] == slots[:, None], slots[None, :], 0), axis=1)
    width = 4096 // n_term
    scratch = [
        pltpu.VMEM((256, 1024), BF16),
        pltpu.VMEM((256, 1024), BF16),
        pltpu.VMEM((4, 256, 256), BF16),
        pltpu.VMEM((256, 64), BF16),
        pltpu.VMEM((256, 64), BF16),
        pltpu.VMEM((2, 128, 256), BF16),
        pltpu.VMEM((2, 128, 256), BF16),
        pltpu.VMEM((256, 256), F32),
        pltpu.VMEM((256, 256), F32),
        pltpu.VMEM((256, 256), F32),
        pltpu.VMEM((256, 256), BF16),
        pltpu.VMEM((256, 256), BF16),
        pltpu.VMEM((4, 256, 1024), BF16),
        pltpu.VMEM((4, 256, 1024), BF16),
        pltpu.VMEM((4, 256, 1024), BF16),
        pltpu.VMEM((2, 4, 128, 1024), BF16),
        pltpu.VMEM((4, 256, 256), BF16),
        pltpu.VMEM((2, 2, 64, 128), BF16),
        pltpu.VMEM((2, 5, 64, 128), BF16),
        pltpu.VMEM((2, 5, 64, 128), BF16),
        pltpu.VMEM((4, 2, 256, 1024), BF16),
        pltpu.VMEM((4, 4, 256, 1024), BF16),
        pltpu.VMEM((8, 64, width), BF16),
        pltpu.VMEM((4, 4, 64, width), BF16),
        pltpu.VMEM((4, 4, 64, width), BF16),
        pltpu.VMEM((4, 64, width), BF16),
        pltpu.VMEM((n_term, 4, 64, width), BF16),
        pltpu.VMEM((n_term, height, 4096), BF16),
        pltpu.VMEM((n_term, height, 4096), BF16),
    ]
    for lead in ((8,), (4, 2), (5, 2)):
        scratch += [pltpu.VMEM(lead + (64, 128), BF16)] * (2 * LEVELS)
    scratch += [dma((count,)) for count in (64, 64, 32, 32, 8, 8, 4, 4, 24, 24, 8, 8)]
    result = pl.pallas_call(
        functools.partial(kernel, n_term),
        out_shape=jax.ShapeDtypeStruct((height, 4096), BF16),
        in_specs=[pl.BlockSpec(memory_space=pltpu.SMEM)] * 3 + [vmem] * 3,
        out_specs=vmem,
        scratch_shapes=scratch,
        compiler_params=pltpu.CompilerParams(
            collective_id=0, has_side_effects=True, vmem_limit_bytes=60 * 1024 * 1024
        ),
    )(node_map, inverse, active[0], node_tensors[0], prim_ops, top_field)
    return result[None]


def solution(mesh):
    placed = (
        P("node", None, None),
        P("node", "term", None, None, None),
        P("node", "term", None),
        P("term", None, None),
        P(),
    )
    return jax.shard_map(
        functools.partial(per_device, mesh.shape["term"]),
        mesh=mesh,
        in_specs=placed,
        out_specs=P("node", "term", None),
        check_vma=False,
    )
```

```python
import functools

import jax
import jax.numpy as jnp
from jax import lax
from jax.experimental import pallas as pl
from jax.experimental.pallas import tpu as pltpu
from jax.sharding import PartitionSpec as P

MESH = pl.DeviceIdType.MESH
F32 = jnp.float32
BF16 = jnp.bfloat16
LEVELS = 4


def mm(x, y):
    return lax.dot_general(x, y, (((1,), (0,)), ((), ())), preferred_element_type=F32)


def mm_nt(x, y):
    return lax.dot_general(x, y, (((1,), (1,)), ((), ())), preferred_element_type=F32)


def iota(shape, dim):
    return lax.broadcasted_iota(jnp.int32, shape, dim)


def kernel(
    n_term,
    node_map,
    inverse,
    active,
    tensor,
    prim,
    top_field,
    out,
    nb,
    swb,
    a3,
    e_r,
    e_l,
    j_r,
    j_l,
    m_r,
    m_l,
    m_m,
    perm,
    unit,
    x_buf,
    y_buf,
    w_buf,
    v_buf,
    bd_buf,
    lr_buf,
    sib_buf,
    m_buf,
    blk,
    sa_buf,
    za,
    pa_send,
    pa,
    ta_send,
    ta,
    pieces,
    rs,
    *rest,
):
    zbuf, psend, prbuf = (rest[8 * k : 8 * k + 8] for k in range(3))
    us, ur, ps, pr, azs, azr, aps, apr, ats, atr, ts, tr = rest[24:36]

    node = lax.axis_index("node")
    term = lax.axis_index("term")
    z = node // 4
    j = lax.rem(node, 4)

    def at_node(zt, jt):
        return {"node": zt * 4 + jt}

    partners = []
    for dz in range(1, 8):
        partners.append(at_node(lax.rem(z + dz, 8), j))
    for dj in range(1, 4):
        partners.append(at_node(z, lax.rem(j + dj, 4)))
    for dt in range(1, n_term):
        partners.append({"term": lax.rem(term + dt, n_term)})
    barrier = pltpu.get_barrier_semaphore()
    for partner in partners:
        pl.semaphore_signal(barrier, inc=1, device_id=partner, device_id_type=MESH)

    rows, cols = iota((256, 64), 0), iota((256, 64), 1)
    by, bx = rows // 16, lax.rem(rows // 4, 4)
    e_r[...] = jnp.where(cols == bx * 16 + by, 1.0, 0.0).astype(BF16)
    e_l[...] = jnp.where(cols == lax.rem(rows, 64), 1.0, 0.0).astype(BF16)
    rows, cols = iota((128, 256), 0), iota((128, 256), 1)
    for half in range(2):
        k = rows - 64 * half
        j_r[half] = jnp.where(k == lax.rem(cols, 64), 1.0, 0.0).astype(BF16)
        j_l[half] = jnp.where(k == lax.rem(cols, 4) * 16 + cols // 16, 1.0, 0.0).astype(BF16)
    rows, cols = iota((256, 256), 0), iota((256, 256), 1)
    m_r[...] = jnp.where(lax.rem(rows, 4) == cols // 64, 1.0, 0.0)
    same_bx = rows // 64 == lax.rem(cols // 4, 4)
    m_l[...] = jnp.where(same_bx, 1.0, 0.0)
    m_m[...] = jnp.where(rows // 64 == cols // 64, 1.0, 0.0)
    same_a = lax.rem(rows, 64) == lax.rem(cols, 4) * 16 + cols // 16
    perm[...] = jnp.where(same_bx & same_a, 1.0, 0.0).astype(BF16)
    same_lo = lax.rem(rows, 4) == cols // 64
    same_t = lax.rem(cols, 64) == lax.rem(rows // 4, 4) * 16 + rows // 16
    unit[...] = jnp.where(same_lo & same_t, 1.0, 0.0).astype(BF16)
    eye = jnp.where(rows == cols, 1.0, 0.0).astype(BF16)
    eye64 = jnp.where(iota((64, 64), 0) == iota((64, 64), 1), 1.0, 0.0).astype(BF16)
    low = iota((16, 128), 1) < 64
    low64 = iota((64, 128), 1) < 64

    def expand(pair, half, e, jm, mask):
        spread = mm(e[...], pair).astype(BF16)
        return (mm(spread, jm[half]) * mask[...]).astype(BF16)

    def spread_mid(weight, src, dst, r):
        for g in range(4):
            o = mm(weight, src(slice(g * 256, g * 256 + 256)))
            for k in range(2):
                for i in range(8):
                    u = o[32 * i : 32 * i + 16, 128 * k : 128 * k + 128]
                    v = o[32 * i + 16 : 32 * i + 32, 128 * k : 128 * k + 128]
                    ur_, vr_ = pltpu.roll(u, 64, 1), pltpu.roll(v, 64, 1)
                    hi = (4 * g + 2 * k) * 16
                    lanes = slice(i * 128, i * 128 + 128)
                    dst[r, hi : hi + 16, lanes] = jnp.where(low, u, vr_).astype(BF16)
                    dst[r, hi + 16 : hi + 32, lanes] = jnp.where(low, ur_, v).astype(BF16)

    def op_on_mid(src, side, dst, hp):
        pair = lr_buf[hp, side]
        for half in range(2):
            weight = expand(pair, half, e_r, j_r, m_r)
            spread_mid(weight, lambda lanes: src[:, lanes], dst, hp * 2 + half)

    def up(send, hp):
        op_on_mid(swb, 1, x_buf, hp)
        pair = lr_buf[hp, 0]
        both = []
        for half in range(2):
            weight = expand(pair, half, e_l, j_l, m_l)
            acc = jnp.zeros((256, 256), F32)
            for g in range(4):
                w = mm(weight, x_buf[hp * 2 + half, :, g * 256 : (g + 1) * 256]).astype(BF16)
                acc = acc + mm(a3[g], w)
            s = jnp.where(low64, acc[0:64, 0:128], acc[64:128, 0:128]) + jnp.where(
                low64, acc[128:192, 128:256], acc[192:256, 128:256]
            )
            both.append(s + pltpu.roll(s, 64, 1))
        send[z] = jnp.where(low64, both[0], both[1]).astype(BF16)

    def natural(src, r, dst):
        for g in range(4):
            lanes = slice(g * 256, g * 256 + 256)
            dst[:, lanes] = mm(perm[...], src[r, :, lanes]).astype(BF16)

    def weighted(hp):
        for half in range(2):
            weight = expand(lr_buf[hp, 0], half, e_l, j_l, m_l)
            r = hp * 2 + half
            for g in range(4):
                lanes = slice(g * 256, g * 256 + 256)
                w_buf[r, :, lanes] = mm(weight, x_buf[r, :, lanes]).astype(BF16)

    def field(k, hp):
        pair = m_buf[hp, k]
        for half in range(2):
            bd_buf[hp * 2 + half] = expand(pair, half, e_l, j_r, m_m)

    def walk(k, hp):
        field(k - 1, hp)
        for half in range(2):
            r = 2 * hp + half
            for g in range(4):
                lanes = slice(g * 256, g * 256 + 256)
                v = mm(sa_buf[k - 1, r, :, lanes], bd_buf[r]).astype(BF16)
                for q in range(4):
                    v_buf[hp, q, half * 64 : half * 64 + 64, lanes] = v[q * 64 : q * 64 + 64]
        acc = jnp.zeros((128, 64), F32)
        for q in range(4):
            acc = acc + mm_nt(v_buf[hp, q], blk[k - 1, base_of[k], q * 64 : q * 64 + 64, :])
        m_buf[hp, k] = jnp.concatenate([acc[0:64], acc[64:128]], axis=1).astype(BF16)

    def prepare(k, hp):
        for half in range(2):
            r = 2 * hp + half
            weight = expand(sib_buf[hp, k], half, e_r, j_r, m_r)
            spread_mid(weight, lambda lanes: blk[k - 1, 1 - base_of[k], :, lanes], y_buf, r)
            natural(y_buf, r, sa_buf.at[k - 1, r])

    for q in range(4):
        nb[q * 64 : q * 64 + 64] = tensor[:, q * 1024 : q * 1024 + 1024]
    for g in range(4):
        a3[g] = mm_nt(eye, nb[:, g * 256 : g * 256 + 256]).astype(BF16)
    y_unit = y_buf
    spread_mid(unit[...], lambda lanes: nb[:, lanes], y_unit, 0)
    natural(y_unit, 0, swb)
    for hp in range(2):
        for side in range(2):
            ops = []
            for r in (2 * hp, 2 * hp + 1):
                acts = jnp.full((64, 64), active[r, side], jnp.int32) == 1
                ops.append(jnp.where(acts, prim[0, r, side], eye64))
            lr_buf[hp, side] = jnp.concatenate(ops, axis=1)
        m_buf[hp, 0] = jnp.concatenate([top_field[2 * hp], top_field[2 * hp + 1]], axis=1)

    def slot_of(q):
        return inverse[jnp.maximum(jnp.minimum(q, 32) - 1, 0)]

    def at_depth(q, k):
        return (q >= 2**k) & (q < 2 ** (k + 1))

    def ancestor(q, k):
        best = jnp.int32(1)
        for up_by in range(6):
            best = jnp.where(at_depth(q // 2**up_by, k), q // 2**up_by, best)
        return best

    def sibling(q):
        return q + 1 - 2 * lax.rem(q, 2)

    here = [node_map[z * 4 + lax.rem(j + k, 4)] + 1 for k in range(4)]
    first_of, second_of, tensors_of = [], [], []
    for q in here:
        first_of.append(
            [
                slot_of(jnp.where(at_depth(q, k - 1), 2 * q, sibling(ancestor(q, k))))
                for k in range(1, 5)
            ]
        )
        second_of.append(slot_of(2 * q + 1))
        tensors_of.append([slot_of(ancestor(q, k)) for k in range(4)])
    base_of = [None] + [lax.rem(ancestor(here[0], k), 2) for k in range(1, 5)]
    depth = jnp.int32(0)
    for k in range(1, 5):
        depth = depth + jnp.where(here[0] >= 2**k, 1, 0)

    pending = []
    flight = {}

    def send(key, sems, slot, src, dst, to):
        copy = pltpu.make_async_remote_copy(
            src_ref=src,
            dst_ref=dst,
            send_sem=sems[0].at[slot],
            recv_sem=sems[1].at[slot],
            device_id=to,
            device_id_type=MESH,
        )
        copy.start()
        flight.setdefault(key, []).append(copy)
        pending.append(copy)

    def arrived(key):
        for copy in flight.pop(key):
            copy.wait_recv()

    def to_ring(dz):
        return at_node(lax.rem(z + dz, 8), j)

    def to_mate(dj):
        return at_node(z, lax.rem(j + dj, 4))

    def up_start(n):
        zb = zbuf[n]
        for dz in (4, 3, 5, 2, 6, 1, 7):
            send(("uz", n), (us, ur), n * 8 + dz, zb.at[z], zb.at[z], to_ring(dz))

    def up_relay(n):
        zb, sb, rb = zbuf[n], psend[n], prbuf[n]
        k = LEVELS - 1 - n // 2
        arrived(("uz", n))
        for dj in (2, 3, 1):
            sb[dj, 0] = zb[first_of[dj][k] // 4]
            sb[dj, 1] = zb[second_of[dj] // 4]
            send(("up", n), (ps, pr), n * 4 + dj, sb.at[dj], rb.at[j], to_mate(dj))
        rb[j, 0] = zb[first_of[0][k] // 4]
        rb[j, 1] = zb[second_of[0] // 4]

    def up_finish(n):
        k, hp = LEVELS - 1 - n // 2, n % 2
        rb = prbuf[n]
        rb[4] = lr_buf[hp]
        arrived(("up", n))
        mine = at_depth(here[0], k)
        first = lax.rem(first_of[0][k], 4)
        lr_buf[hp, 0] = rb[jnp.where(mine, first, 4), 0]
        lr_buf[hp, 1] = rb[jnp.where(mine, lax.rem(second_of[0], 4), 4), 1]
        sib_buf[hp, k + 1] = rb[first, 0]

    width = 4096 // n_term
    per_block = 1024 // width

    def fetch_start():
        mine = tensor.at[:, pl.ds(pl.multiple_of(term * width, width), width)]
        for dz in (4, 3, 5, 2, 6, 1, 7):
            send("az", (azs, azr), dz, mine, za.at[z], to_ring(dz))
        za[z] = tensor[:, pl.ds(pl.multiple_of(term * width, width), width)]

    def fetch_relay():
        arrived("az")
        for dj in (2, 3, 1):
            for k in range(4):
                pa_send[dj, k] = za[tensors_of[dj][k] // 4]
            send("ap", (aps, apr), dj, pa_send.at[dj], pa.at[j], to_mate(dj))
        for k in range(4):
            pa[j, k] = za[tensors_of[0][k] // 4]

    def fetch_share():
        arrived("ap")
        for k in range(4):
            ta_send[k] = pa[lax.rem(tensors_of[0][k], 4), k]
        send("ax", (ats, atr), 0, ta_send, ta.at[4], {"term": lax.rem(term + 4, 8)})
        fetch_along(0, ta_send)

    row, column = term // 4, lax.rem(term, 4)

    def fetch_along(first, source):
        for part in (1, 0):
            cut = pl.ds(2 * part, 2)
            for dy in (2, 1, 3):
                to = {"term": row * 4 + lax.rem(column + dy, 4)}
                slot = 8 * part + 8 + first + dy
                send(("at", part), (ats, atr), slot, source.at[cut], ta.at[first + dy, cut], to)

    def fetch_spread():
        arrived("ax")
        fetch_along(4, ta.at[4])

    def fetch_finish(part):
        arrived(("at", part))
        for dt in range(8):
            source = lax.rem(row + dt // 4, 2) * 4 + lax.rem(column - dt % 4 + 4, 4)
            rows_at = pl.ds(pl.multiple_of((source // per_block) * 64, 64), 64)
            lanes_at = pl.ds(pl.multiple_of(lax.rem(source, per_block) * width, width), width)
            for k in (2 * part, 2 * part + 1):
                blk[k, 0, rows_at, lanes_at] = ta_send[k] if dt == 0 else ta[dt, k]

        def swap(k, _):
            spread_mid(unit[...], lambda lanes: blk[k, 0, :, lanes], y_buf, 0)
            natural(y_buf, 0, blk.at[k, 1])
            return 0

        lax.fori_loop(2 * part, 2 * part + 2, swap, 0)

    for level in range(LEVELS):
        for hp in range(2):
            n = 2 * level + hp
            if level > 0:
                up_finish(n - 2)
            up(zbuf[n], hp)
            if level > 0:
                up_start(n)
        if level == 0:
            pl.semaphore_wait(barrier, len(partners))
            up_start(0)
            up_start(1)
            fetch_start()
        if level == 2:
            fetch_spread()
        if level == 3:
            fetch_finish(1)
            for hp in range(2):
                prepare(4, hp)
        up_relay(2 * level)
        up_relay(2 * level + 1)
        if level == 0:
            fetch_relay()
        if level == 1:
            fetch_share()
        if level == 3:
            for hp in range(2):
                prepare(3, hp)
            fetch_finish(0)
            for hp in range(2):
                prepare(2, hp)

    for hp in range(2):
        up_finish(2 * LEVELS - 2 + hp)
        prepare(1, hp)
        op_on_mid(swb, 1, x_buf, hp)
        weighted(hp)
    for k in range(1, 5):
        for hp in range(2):
            walk(k, hp)
    for hp in range(2):
        field(depth, hp)
    height = 64 // n_term

    def last(g, _):
        lanes = pl.ds(pl.multiple_of(g * 256, 256), 256)
        acc = jnp.zeros((256, 256), F32)
        for r in range(4):
            acc = acc + mm(w_buf[r, :, lanes], bd_buf[r])
        for q in range(4):
            span = pl.ds(pl.multiple_of(q * 1024 + g * 256, 256), 256)
            for t in range(n_term):
                first = q * 64 + t * height
                pieces[t, :, span] = acc[first : first + height].astype(BF16)
        return 0

    lax.fori_loop(0, 4, last, 0)
    for dt in range(1, n_term):
        target = lax.rem(term + dt, n_term)
        send("t", (ts, tr), dt, pieces.at[target], rs.at[dt], {"term": target})
    total = pieces[term].astype(F32)
    if n_term > 1:
        arrived("t")
    for dt in range(1, n_term):
        total = total + rs[dt].astype(F32)
    absent = jnp.full(total.shape, here[0], jnp.int32) == 32
    out[...] = jnp.where(absent, 0.0, total).astype(BF16)
    for copy in pending:
        copy.wait_send()


def per_device(n_term, node_tensors, prim_ops, active, top_field, node_map):
    vmem = pl.BlockSpec(memory_space=pltpu.VMEM)
    height = 64 // n_term
    dma = pltpu.SemaphoreType.DMA
    slots = jnp.arange(32, dtype=jnp.int32)
    inverse = jnp.sum(jnp.where(node_map[None, :] == slots[:, None], slots[None, :], 0), axis=1)
    width = 4096 // n_term
    scratch = [
        pltpu.VMEM((256, 1024), BF16),
        pltpu.VMEM((256, 1024), BF16),
        pltpu.VMEM((4, 256, 256), BF16),
        pltpu.VMEM((256, 64), BF16),
        pltpu.VMEM((256, 64), BF16),
        pltpu.VMEM((2, 128, 256), BF16),
        pltpu.VMEM((2, 128, 256), BF16),
        pltpu.VMEM((256, 256), F32),
        pltpu.VMEM((256, 256), F32),
        pltpu.VMEM((256, 256), F32),
        pltpu.VMEM((256, 256), BF16),
        pltpu.VMEM((256, 256), BF16),
        pltpu.VMEM((4, 256, 1024), BF16),
        pltpu.VMEM((4, 256, 1024), BF16),
        pltpu.VMEM((4, 256, 1024), BF16),
        pltpu.VMEM((2, 4, 128, 1024), BF16),
        pltpu.VMEM((4, 256, 256), BF16),
        pltpu.VMEM((2, 2, 64, 128), BF16),
        pltpu.VMEM((2, 5, 64, 128), BF16),
        pltpu.VMEM((2, 5, 64, 128), BF16),
        pltpu.VMEM((4, 2, 256, 1024), BF16),
        pltpu.VMEM((4, 4, 256, 1024), BF16),
        pltpu.VMEM((8, 64, width), BF16),
        pltpu.VMEM((4, 4, 64, width), BF16),
        pltpu.VMEM((4, 4, 64, width), BF16),
        pltpu.VMEM((4, 64, width), BF16),
        pltpu.VMEM((n_term, 4, 64, width), BF16),
        pltpu.VMEM((n_term, height, 4096), BF16),
        pltpu.VMEM((n_term, height, 4096), BF16),
    ]
    for lead in ((8,), (4, 2), (5, 2)):
        scratch += [pltpu.VMEM(lead + (64, 128), BF16)] * (2 * LEVELS)
    scratch += [dma((count,)) for count in (64, 64, 32, 32, 8, 8, 4, 4, 24, 24, 8, 8)]
    result = pl.pallas_call(
        functools.partial(kernel, n_term),
        out_shape=jax.ShapeDtypeStruct((height, 4096), BF16),
        in_specs=[pl.BlockSpec(memory_space=pltpu.SMEM)] * 3 + [vmem] * 3,
        out_specs=vmem,
        scratch_shapes=scratch,
        compiler_params=pltpu.CompilerParams(
            collective_id=0, has_side_effects=True, vmem_limit_bytes=60 * 1024 * 1024
        ),
    )(node_map, inverse, active[0], node_tensors[0], prim_ops, top_field)
    return result[None]


def solution(mesh):
    placed = (
        P("node", None, None),
        P("node", "term", None, None, None),
        P("node", "term", None),
        P("term", None, None),
        P(),
    )
    return jax.shard_map(
        functools.partial(per_device, mesh.shape["term"]),
        mesh=mesh,
        in_specs=placed,
        out_specs=P("node", "term", None),
        check_vma=False,
    )
```

```python
import functools

import jax
import jax.numpy as jnp
from jax import lax
from jax.experimental import pallas as pl
from jax.experimental.pallas import tpu as pltpu
from jax.sharding import PartitionSpec as P

MESH = pl.DeviceIdType.MESH
F32 = jnp.float32
BF16 = jnp.bfloat16
LEVELS = 4


def mm(x, y):
    return lax.dot_general(x, y, (((1,), (0,)), ((), ())), preferred_element_type=F32)


def mm_nt(x, y):
    return lax.dot_general(x, y, (((1,), (1,)), ((), ())), preferred_element_type=F32)


def iota(shape, dim):
    return lax.broadcasted_iota(jnp.int32, shape, dim)


def kernel(
    n_term,
    node_map,
    inverse,
    active,
    tensor,
    prim,
    top_field,
    out,
    nb,
    swb,
    a3,
    e_r,
    e_l,
    j_r,
    j_l,
    m_r,
    m_l,
    m_m,
    perm,
    unit,
    x_buf,
    y_buf,
    w_buf,
    v_buf,
    bd_buf,
    lr_buf,
    sib_buf,
    m_buf,
    blk,
    sa_buf,
    za,
    pa_send,
    pa,
    ta_send,
    ta,
    pieces,
    rs,
    *rest,
):
    zbuf, psend, prbuf = (rest[8 * k : 8 * k + 8] for k in range(3))
    us, ur, ps, pr, azs, azr, aps, apr, ats, atr, ts, tr = rest[24:36]

    node = lax.axis_index("node")
    term = lax.axis_index("term")
    z = node // 4
    j = lax.rem(node, 4)

    def at_node(zt, jt):
        return {"node": zt * 4 + jt}

    partners = []
    for dz in range(1, 8):
        partners.append(at_node(lax.rem(z + dz, 8), j))
    for dj in range(1, 4):
        partners.append(at_node(z, lax.rem(j + dj, 4)))
    for dt in range(1, n_term):
        partners.append({"term": lax.rem(term + dt, n_term)})
    barrier = pltpu.get_barrier_semaphore()
    for partner in partners:
        pl.semaphore_signal(barrier, inc=1, device_id=partner, device_id_type=MESH)

    rows, cols = iota((256, 64), 0), iota((256, 64), 1)
    by, bx = rows // 16, lax.rem(rows // 4, 4)
    e_r[...] = jnp.where(cols == bx * 16 + by, 1.0, 0.0).astype(BF16)
    e_l[...] = jnp.where(cols == lax.rem(rows, 64), 1.0, 0.0).astype(BF16)
    rows, cols = iota((128, 256), 0), iota((128, 256), 1)
    for half in range(2):
        k = rows - 64 * half
        j_r[half] = jnp.where(k == lax.rem(cols, 64), 1.0, 0.0).astype(BF16)
        j_l[half] = jnp.where(k == lax.rem(cols, 4) * 16 + cols // 16, 1.0, 0.0).astype(BF16)
    rows, cols = iota((256, 256), 0), iota((256, 256), 1)
    m_r[...] = jnp.where(lax.rem(rows, 4) == cols // 64, 1.0, 0.0)
    same_bx = rows // 64 == lax.rem(cols // 4, 4)
    m_l[...] = jnp.where(same_bx, 1.0, 0.0)
    m_m[...] = jnp.where(rows // 64 == cols // 64, 1.0, 0.0)
    same_a = lax.rem(rows, 64) == lax.rem(cols, 4) * 16 + cols // 16
    perm[...] = jnp.where(same_bx & same_a, 1.0, 0.0).astype(BF16)
    same_lo = lax.rem(rows, 4) == cols // 64
    same_t = lax.rem(cols, 64) == lax.rem(rows // 4, 4) * 16 + rows // 16
    unit[...] = jnp.where(same_lo & same_t, 1.0, 0.0).astype(BF16)
    eye = jnp.where(rows == cols, 1.0, 0.0).astype(BF16)
    eye64 = jnp.where(iota((64, 64), 0) == iota((64, 64), 1), 1.0, 0.0).astype(BF16)
    low = iota((16, 128), 1) < 64
    low64 = iota((64, 128), 1) < 64

    def expand(pair, half, e, jm, mask):
        spread = mm(e[...], pair).astype(BF16)
        return (mm(spread, jm[half]) * mask[...]).astype(BF16)

    def spread_mid(weight, src, dst, r):
        for g in range(4):
            o = mm(weight, src(slice(g * 256, g * 256 + 256)))
            for k in range(2):
                for i in range(8):
                    u = o[32 * i : 32 * i + 16, 128 * k : 128 * k + 128]
                    v = o[32 * i + 16 : 32 * i + 32, 128 * k : 128 * k + 128]
                    ur_, vr_ = pltpu.roll(u, 64, 1), pltpu.roll(v, 64, 1)
                    hi = (4 * g + 2 * k) * 16
                    lanes = slice(i * 128, i * 128 + 128)
                    dst[r, hi : hi + 16, lanes] = jnp.where(low, u, vr_).astype(BF16)
                    dst[r, hi + 16 : hi + 32, lanes] = jnp.where(low, ur_, v).astype(BF16)

    def op_on_mid(src, side, dst, hp):
        pair = lr_buf[hp, side]
        for half in range(2):
            weight = expand(pair, half, e_r, j_r, m_r)
            spread_mid(weight, lambda lanes: src[:, lanes], dst, hp * 2 + half)

    def up(send, hp):
        op_on_mid(swb, 1, x_buf, hp)
        pair = lr_buf[hp, 0]
        both = []
        for half in range(2):
            weight = expand(pair, half, e_l, j_l, m_l)
            acc = jnp.zeros((256, 256), F32)
            for g in range(4):
                w = mm(weight, x_buf[hp * 2 + half, :, g * 256 : (g + 1) * 256]).astype(BF16)
                acc = acc + mm(a3[g], w)
            s = jnp.where(low64, acc[0:64, 0:128], acc[64:128, 0:128]) + jnp.where(
                low64, acc[128:192, 128:256], acc[192:256, 128:256]
            )
            both.append(s + pltpu.roll(s, 64, 1))
        send[z] = jnp.where(low64, both[0], both[1]).astype(BF16)

    def natural(src, r, dst):
        for g in range(4):
            lanes = slice(g * 256, g * 256 + 256)
            dst[:, lanes] = mm(perm[...], src[r, :, lanes]).astype(BF16)

    def weighted(hp):
        for half in range(2):
            weight = expand(lr_buf[hp, 0], half, e_l, j_l, m_l)
            r = hp * 2 + half
            for g in range(4):
                lanes = slice(g * 256, g * 256 + 256)
                w_buf[r, :, lanes] = mm(weight, x_buf[r, :, lanes]).astype(BF16)

    def field(k, hp):
        pair = m_buf[hp, k]
        for half in range(2):
            bd_buf[hp * 2 + half] = expand(pair, half, e_l, j_r, m_m)

    def walk(k, hp):
        field(k - 1, hp)
        for half in range(2):
            r = 2 * hp + half
            for g in range(4):
                lanes = slice(g * 256, g * 256 + 256)
                v = mm(sa_buf[k - 1, r, :, lanes], bd_buf[r]).astype(BF16)
                for q in range(4):
                    v_buf[hp, q, half * 64 : half * 64 + 64, lanes] = v[q * 64 : q * 64 + 64]
        acc = jnp.zeros((128, 64), F32)
        for q in range(4):
            acc = acc + mm_nt(v_buf[hp, q], blk[k - 1, base_of[k], q * 64 : q * 64 + 64, :])
        m_buf[hp, k] = jnp.concatenate([acc[0:64], acc[64:128]], axis=1).astype(BF16)

    def prepare(k, hp):
        for half in range(2):
            r = 2 * hp + half
            weight = expand(sib_buf[hp, k], half, e_r, j_r, m_r)
            spread_mid(weight, lambda lanes: blk[k - 1, 1 - base_of[k], :, lanes], y_buf, r)
            natural(y_buf, r, sa_buf.at[k - 1, r])

    for q in range(4):
        nb[q * 64 : q * 64 + 64] = tensor[:, q * 1024 : q * 1024 + 1024]
    for g in range(4):
        a3[g] = mm_nt(eye, nb[:, g * 256 : g * 256 + 256]).astype(BF16)
    y_unit = y_buf
    spread_mid(unit[...], lambda lanes: nb[:, lanes], y_unit, 0)
    natural(y_unit, 0, swb)
    for hp in range(2):
        for side in range(2):
            ops = []
            for r in (2 * hp, 2 * hp + 1):
                acts = jnp.full((64, 64), active[r, side], jnp.int32) == 1
                ops.append(jnp.where(acts, prim[0, r, side], eye64))
            lr_buf[hp, side] = jnp.concatenate(ops, axis=1)
        m_buf[hp, 0] = jnp.concatenate([top_field[2 * hp], top_field[2 * hp + 1]], axis=1)

    def slot_of(q):
        return inverse[jnp.maximum(jnp.minimum(q, 32) - 1, 0)]

    def at_depth(q, k):
        return (q >= 2**k) & (q < 2 ** (k + 1))

    def ancestor(q, k):
        best = jnp.int32(1)
        for up_by in range(6):
            best = jnp.where(at_depth(q // 2**up_by, k), q // 2**up_by, best)
        return best

    def sibling(q):
        return q + 1 - 2 * lax.rem(q, 2)

    here = [node_map[z * 4 + lax.rem(j + k, 4)] + 1 for k in range(4)]
    first_of, second_of, tensors_of = [], [], []
    for q in here:
        first_of.append(
            [
                slot_of(jnp.where(at_depth(q, k - 1), 2 * q, sibling(ancestor(q, k))))
                for k in range(1, 5)
            ]
        )
        second_of.append(slot_of(2 * q + 1))
        tensors_of.append([slot_of(ancestor(q, k)) for k in range(4)])
    base_of = [None] + [lax.rem(ancestor(here[0], k), 2) for k in range(1, 5)]
    depth = jnp.int32(0)
    for k in range(1, 5):
        depth = depth + jnp.where(here[0] >= 2**k, 1, 0)

    pending = []
    flight = {}

    def send(key, sems, slot, src, dst, to):
        copy = pltpu.make_async_remote_copy(
            src_ref=src,
            dst_ref=dst,
            send_sem=sems[0].at[slot],
            recv_sem=sems[1].at[slot],
            device_id=to,
            device_id_type=MESH,
        )
        copy.start()
        flight.setdefault(key, []).append(copy)
        pending.append(copy)

    def arrived(key):
        for copy in flight.pop(key):
            copy.wait_recv()

    def to_ring(dz):
        return at_node(lax.rem(z + dz, 8), j)

    def to_mate(dj):
        return at_node(z, lax.rem(j + dj, 4))

    def up_start(n):
        zb = zbuf[n]
        for dz in (4, 3, 5, 2, 6, 1, 7):
            send(("uz", n), (us, ur), n * 8 + dz, zb.at[z], zb.at[z], to_ring(dz))

    def up_relay(n):
        zb, sb, rb = zbuf[n], psend[n], prbuf[n]
        k = LEVELS - 1 - n // 2
        arrived(("uz", n))
        for dj in (2, 3, 1):
            sb[dj, 0] = zb[first_of[dj][k] // 4]
            sb[dj, 1] = zb[second_of[dj] // 4]
            send(("up", n), (ps, pr), n * 4 + dj, sb.at[dj], rb.at[j], to_mate(dj))
        rb[j, 0] = zb[first_of[0][k] // 4]
        rb[j, 1] = zb[second_of[0] // 4]

    def up_finish(n):
        k, hp = LEVELS - 1 - n // 2, n % 2
        rb = prbuf[n]
        rb[4] = lr_buf[hp]
        arrived(("up", n))
        mine = at_depth(here[0], k)
        first = lax.rem(first_of[0][k], 4)
        lr_buf[hp, 0] = rb[jnp.where(mine, first, 4), 0]
        lr_buf[hp, 1] = rb[jnp.where(mine, lax.rem(second_of[0], 4), 4), 1]
        sib_buf[hp, k + 1] = rb[first, 0]

    width = 4096 // n_term
    per_block = 1024 // width

    def fetch_start():
        mine = tensor.at[:, pl.ds(pl.multiple_of(term * width, width), width)]
        for dz in (4, 3, 5, 2, 6, 1, 7):
            send("az", (azs, azr), dz, mine, za.at[z], to_ring(dz))
        za[z] = tensor[:, pl.ds(pl.multiple_of(term * width, width), width)]

    def fetch_relay():
        arrived("az")
        for dj in (2, 3, 1):
            for k in range(4):
                pa_send[dj, k] = za[tensors_of[dj][k] // 4]
            send("ap", (aps, apr), dj, pa_send.at[dj], pa.at[j], to_mate(dj))
        for k in range(4):
            pa[j, k] = za[tensors_of[0][k] // 4]

    def fetch_share():
        arrived("ap")
        for k in range(4):
            ta_send[k] = pa[lax.rem(tensors_of[0][k], 4), k]
        send("ax", (ats, atr), 0, ta_send, ta.at[4], {"term": lax.rem(term + 4, 8)})
        fetch_along(0, ta_send)

    row, column = term // 4, lax.rem(term, 4)

    def fetch_along(first, source):
        for part in (1, 0):
            cut = pl.ds(2 * part, 2)
            for dy in (2, 1, 3):
                to = {"term": row * 4 + lax.rem(column + dy, 4)}
                slot = 8 * part + 8 + first + dy
                send(("at", part), (ats, atr), slot, source.at[cut], ta.at[first + dy, cut], to)

    def fetch_spread():
        arrived("ax")
        fetch_along(4, ta.at[4])

    def fetch_finish(part):
        arrived(("at", part))
        for dt in range(8):
            source = lax.rem(row + dt // 4, 2) * 4 + lax.rem(column - dt % 4 + 4, 4)
            rows_at = pl.ds(pl.multiple_of((source // per_block) * 64, 64), 64)
            lanes_at = pl.ds(pl.multiple_of(lax.rem(source, per_block) * width, width), width)
            for k in (2 * part, 2 * part + 1):
                blk[k, 0, rows_at, lanes_at] = ta_send[k] if dt == 0 else ta[dt, k]

        def swap(k, _):
            spread_mid(unit[...], lambda lanes: blk[k, 0, :, lanes], y_buf, 0)
            natural(y_buf, 0, blk.at[k, 1])
            return 0

        lax.fori_loop(2 * part, 2 * part + 2, swap, 0)

    for level in range(LEVELS):
        for hp in range(2):
            n = 2 * level + hp
            if level > 0:
                up_finish(n - 2)
            up(zbuf[n], hp)
            if level > 0:
                up_start(n)
        if level == 0:
            pl.semaphore_wait(barrier, len(partners))
            up_start(0)
            up_start(1)
            fetch_start()
        if level == 2:
            fetch_spread()
        if level == 3:
            fetch_finish(1)
            for hp in range(2):
                prepare(4, hp)
        up_relay(2 * level)
        if level == 3:
            prepare(3, 0)
        up_relay(2 * level + 1)
        if level == 0:
            fetch_relay()
        if level == 1:
            fetch_share()
        if level == 3:
            prepare(3, 1)
            fetch_finish(0)

    def own_weighted(hp):
        op_on_mid(swb, 1, x_buf, hp)
        weighted(hp)

    for hp in range(2):
        up_finish(2 * LEVELS - 2 + hp)
        prepare(1, hp)
        walk(1, hp)
        prepare(2, hp)
    walk(2, 0)
    own_weighted(0)
    walk(2, 1)
    walk(3, 0)
    own_weighted(1)
    walk(3, 1)
    walk(4, 0)
    walk(4, 1)
    for hp in range(2):
        field(depth, hp)
    height = 64 // n_term

    def last(g, _):
        lanes = pl.ds(pl.multiple_of(g * 256, 256), 256)
        acc = jnp.zeros((256, 256), F32)
        for r in range(4):
            acc = acc + mm(w_buf[r, :, lanes], bd_buf[r])
        for q in range(4):
            span = pl.ds(pl.multiple_of(q * 1024 + g * 256, 256), 256)
            for t in range(n_term):
                first = q * 64 + t * height
                pieces[t, :, span] = acc[first : first + height].astype(BF16)
        return 0

    lax.fori_loop(0, 4, last, 0)
    for dt in range(1, n_term):
        target = lax.rem(term + dt, n_term)
        send("t", (ts, tr), dt, pieces.at[target], rs.at[dt], {"term": target})
    total = pieces[term].astype(F32)
    if n_term > 1:
        arrived("t")
    for dt in range(1, n_term):
        total = total + rs[dt].astype(F32)
    absent = jnp.full(total.shape, here[0], jnp.int32) == 32
    out[...] = jnp.where(absent, 0.0, total).astype(BF16)
    for copy in pending:
        copy.wait_send()


def per_device(n_term, node_tensors, prim_ops, active, top_field, node_map):
    vmem = pl.BlockSpec(memory_space=pltpu.VMEM)
    height = 64 // n_term
    dma = pltpu.SemaphoreType.DMA
    slots = jnp.arange(32, dtype=jnp.int32)
    inverse = jnp.sum(jnp.where(node_map[None, :] == slots[:, None], slots[None, :], 0), axis=1)
    width = 4096 // n_term
    scratch = [
        pltpu.VMEM((256, 1024), BF16),
        pltpu.VMEM((256, 1024), BF16),
        pltpu.VMEM((4, 256, 256), BF16),
        pltpu.VMEM((256, 64), BF16),
        pltpu.VMEM((256, 64), BF16),
        pltpu.VMEM((2, 128, 256), BF16),
        pltpu.VMEM((2, 128, 256), BF16),
        pltpu.VMEM((256, 256), F32),
        pltpu.VMEM((256, 256), F32),
        pltpu.VMEM((256, 256), F32),
        pltpu.VMEM((256, 256), BF16),
        pltpu.VMEM((256, 256), BF16),
        pltpu.VMEM((4, 256, 1024), BF16),
        pltpu.VMEM((4, 256, 1024), BF16),
        pltpu.VMEM((4, 256, 1024), BF16),
        pltpu.VMEM((2, 4, 128, 1024), BF16),
        pltpu.VMEM((4, 256, 256), BF16),
        pltpu.VMEM((2, 2, 64, 128), BF16),
        pltpu.VMEM((2, 5, 64, 128), BF16),
        pltpu.VMEM((2, 5, 64, 128), BF16),
        pltpu.VMEM((4, 2, 256, 1024), BF16),
        pltpu.VMEM((4, 4, 256, 1024), BF16),
        pltpu.VMEM((8, 64, width), BF16),
        pltpu.VMEM((4, 4, 64, width), BF16),
        pltpu.VMEM((4, 4, 64, width), BF16),
        pltpu.VMEM((4, 64, width), BF16),
        pltpu.VMEM((n_term, 4, 64, width), BF16),
        pltpu.VMEM((n_term, height, 4096), BF16),
        pltpu.VMEM((n_term, height, 4096), BF16),
    ]
    for lead in ((8,), (4, 2), (5, 2)):
        scratch += [pltpu.VMEM(lead + (64, 128), BF16)] * (2 * LEVELS)
    scratch += [dma((count,)) for count in (64, 64, 32, 32, 8, 8, 4, 4, 24, 24, 8, 8)]
    result = pl.pallas_call(
        functools.partial(kernel, n_term),
        out_shape=jax.ShapeDtypeStruct((height, 4096), BF16),
        in_specs=[pl.BlockSpec(memory_space=pltpu.SMEM)] * 3 + [vmem] * 3,
        out_specs=vmem,
        scratch_shapes=scratch,
        compiler_params=pltpu.CompilerParams(
            collective_id=0, has_side_effects=True, vmem_limit_bytes=60 * 1024 * 1024
        ),
    )(node_map, inverse, active[0], node_tensors[0], prim_ops, top_field)
    return result[None]


def solution(mesh):
    placed = (
        P("node", None, None),
        P("node", "term", None, None, None),
        P("node", "term", None),
        P("term", None, None),
        P(),
    )
    return jax.shard_map(
        functools.partial(per_device, mesh.shape["term"]),
        mesh=mesh,
        in_specs=placed,
        out_specs=P("node", "term", None),
        check_vma=False,
    )
```
